256 devices in a mesh: blk: 128 (over z, y, x), chan: 2 (over core).
Axes of the slice: x: 4, y: 4, z: 8, core: 2. Of those that a mesh axis runs over, the one named last changes fastest.
Arguments:
- inputs: bfloat16 [128, 512, 512], P('chan', 'blk'), may hold values from -6 to 6
- w_first: bfloat16 [3, 3, 128, 128], P(None, None, 'chan'), may hold values from -0.1875 to 0.1875
- w_second: bfloat16 [3, 3, 128, 128], P(None, None, 'chan'), may hold values from -0.1875 to 0.1875
- w_third: bfloat16 [3, 3, 256, 128], P(None, None, 'chan'), may hold values from -0.1875 to 0.1875
- cotangent: bfloat16 [256, 256, 256], P('chan', 'blk'), may hold values from -6 to 6
- mirror: int32 [128], P('blk'), may hold values from 0 to 1
Outputs:
- grad_inputs: bfloat16 [128, 512, 512], P('chan', 'blk')
- grad_first: float32 [3, 3, 128, 128], P(None, None, 'chan')
- grad_second: float32 [3, 3, 128, 128], P(None, None, 'chan')
- grad_third: float32 [3, 3, 256, 128], P(None, None, 'chan')
The draws below stay inside these ranges and needn't reach their ends.
Inputs may be any that keep to these rules, and one draw needn't show every extreme that they name: `mirror`: 1 marks a tile whose columns are stored in reverse order, 0 a tile stored in the cycle's order.
All inputs are finite; a program needn't handle non-finite values.
Results may differ from the reference program's by a relative error of at most 0.024.
Values may be sent and summed in bfloat16 or wider, within the bound.
A program may use at most 64 MiB of HBM per device.

```python
import math
import jax
import jax.numpy as jnp

C = 128
C2 = 256
COLS = 512
TILES = 128
CYCLE = 512


def set_ends(array, stream_key, low, largest):
    shape = array.shape
    place = [jax.random.randint(jax.random.fold_in(stream_key, axis), (), 0, shape[axis]) for axis in range(len(shape))]
    array = array.at[tuple(place)].set(low)
    longest = shape.index(max(shape))
    place[longest] = (place[longest] + 1) % shape[longest]
    return array.at[tuple(place)].set(largest)


def levels(rng, dims, split, smallest, top_value):
    loudness = 1.0
    for axis_at, blocks in split:
        heights = jax.random.uniform(jax.random.fold_in(jax.random.fold_in(rng, 6), axis_at), (blocks,), jnp.float32, smallest / len(split), top_value / len(split))
        loudness = loudness * jnp.repeat(jnp.exp(heights), dims[axis_at] // blocks).reshape((-1,) + (1,) * (len(dims) - 1 - axis_at))
    return loudness


def scatter_about(rng, extent, scale, bound, cuts=(), kind=jnp.bfloat16):
    gain = levels(rng, extent, cuts, -0.22, 0.18) if cuts else 1.0
    values = jax.random.normal(rng, extent, jnp.float32) * scale * gain
    return jnp.minimum(jnp.maximum(values, -bound), bound).astype(kind)


def setup_inputs(seed: int = 0) -> dict:
    streams_of = jax.random.split(jax.random.key(seed), 7)
    inputs = scatter_about(streams_of[0], (C, CYCLE, COLS), 1.0, 6.0, ((0, 2), (1, 128)))
    w_first = scatter_about(streams_of[1], (3, 3, C, C), (9 * C) ** -0.5, 0.1875, ((2, 2),))
    w_second = scatter_about(streams_of[2], (3, 3, C, C), (9 * C) ** -0.5, 0.1875, ((2, 2),))
    w_third = scatter_about(streams_of[3], (3, 3, C2, C), (9 * C) ** -0.5, 0.1875, ((2, 2),))
    cotangent = scatter_about(streams_of[4], (C2, CYCLE // 2, COLS // 2), 1.0, 6.0, ((0, 2), (1, 128)))
    mirror = set_ends(jax.random.randint(streams_of[5], (TILES,), 0, 2), jax.random.fold_in(streams_of[5], 1), 0, 1).astype(jnp.int32)
    return dict(inputs=inputs, w_first=w_first, w_second=w_second, w_third=w_third, cotangent=cotangent, mirror=mirror)


def orient(field, mirror):
    channels, cycle_rows, columns = field.shape
    tiles = mirror.shape[0]
    blocks = field.reshape(channels, tiles, cycle_rows // tiles, columns)
    turned = jnp.where(mirror[None, :, None, None] == 1, blocks[..., ::-1], blocks)
    return turned.reshape(channels, cycle_rows, columns)

def wrap_rows(field):
    return jnp.concatenate([field[:, -1:], field, field[:, :1]], axis=1)

def conv_taps(padded, weight):
    row_count = padded.shape[1] - 2
    col_count = padded.shape[2]
    framed = jnp.pad(padded, ((0, 0), (0, 0), (1, 1)))
    running = jnp.zeros((weight.shape[2], row_count, col_count), jnp.float32)
    for row_tap in range(3):
        for col_tap in range(3):
            running = running + jnp.einsum('oi,irw->orw', weight[row_tap, col_tap].astype(jnp.float32), framed[:, row_tap:row_tap + row_count, col_tap:col_tap + col_count])
    return running

def weight_taps(grad_out, padded):
    row_count = grad_out.shape[1]
    col_count = grad_out.shape[2]
    framed = jnp.pad(padded, ((0, 0), (0, 0), (1, 1)))
    stacked = []
    for row_tap in range(3):
        line = []
        for col_tap in range(3):
            line.append(jnp.einsum('orw,irw->oi', grad_out, framed[:, row_tap:row_tap + row_count, col_tap:col_tap + col_count]))
        stacked.append(jnp.stack(line))
    return jnp.stack(stacked)

def spread_taps(grad_out, weight):
    row_count = grad_out.shape[1]
    col_count = grad_out.shape[2]
    running = jnp.zeros((weight.shape[3], row_count + 2, col_count + 2), jnp.float32)
    for row_tap in range(3):
        for col_tap in range(3):
            term = jnp.einsum('oi,orw->irw', weight[row_tap, col_tap].astype(jnp.float32), grad_out)
            running = running.at[:, row_tap:row_tap + row_count, col_tap:col_tap + col_count].add(term)
    return running[:, :, 1:-1]

def stride_framed(field):
    stacked = jnp.concatenate([field[:, -1:], field], axis=1)
    return jnp.pad(stacked, ((0, 0), (0, 0), (1, 0)))

def reference(inputs, w_first, w_second, w_third, cotangent, mirror):
    cycle_rows = inputs.shape[1]
    col_count = inputs.shape[2]
    oriented = orient(inputs, mirror)
    upstream = orient(cotangent, mirror).astype(jnp.float32)
    first_pad = wrap_rows(oriented).astype(jnp.float32)
    first_pre = conv_taps(first_pad, w_first)
    first_act = jax.nn.gelu(first_pre).astype(jnp.bfloat16)
    second_pad = wrap_rows(first_act).astype(jnp.float32)
    second_pre = conv_taps(second_pad, w_second)
    second_act = jax.nn.gelu(second_pre).astype(jnp.bfloat16)
    out_rows = upstream.shape[1]
    out_cols = upstream.shape[2]
    framed = stride_framed(second_act.astype(jnp.float32))
    stacked = []
    for row_tap in range(3):
        line = []
        for col_tap in range(3):
            line.append(jnp.einsum('orw,irw->oi', upstream, framed[:, row_tap:row_tap + 2 * out_rows:2, col_tap:col_tap + 2 * out_cols:2]))
        stacked.append(jnp.stack(line))
    third_grad = jnp.stack(stacked)
    running = jnp.zeros((w_third.shape[3], cycle_rows + 1, col_count + 1), jnp.float32)
    for row_tap in range(3):
        for col_tap in range(3):
            term = jnp.einsum('oi,orw->irw', w_third[row_tap, col_tap].astype(jnp.float32), upstream)
            running = running.at[:, row_tap:row_tap + 2 * out_rows:2, col_tap:col_tap + 2 * out_cols:2].add(term)
    running = running[:, :, 1:]
    second_back = running[:, 1:].at[:, -1:].add(running[:, :1])
    second_delta = jax.vjp(jax.nn.gelu, second_pre)[1](second_back)[0].astype(jnp.bfloat16)
    second_delta_f = second_delta.astype(jnp.float32)
    second_grad = weight_taps(second_delta_f, second_pad)
    spread = spread_taps(second_delta_f, w_second)
    first_back = spread[:, 1:-1].at[:, -1:].add(spread[:, :1])
    first_back = first_back.at[:, :1].add(spread[:, -1:])
    first_delta = jax.vjp(jax.nn.gelu, first_pre)[1](first_back)[0].astype(jnp.bfloat16)
    first_delta_f = first_delta.astype(jnp.float32)
    first_grad = weight_taps(first_delta_f, first_pad)
    spread = spread_taps(first_delta_f, w_first)
    input_back = spread[:, 1:-1].at[:, -1:].add(spread[:, :1])
    input_back = input_back.at[:, :1].add(spread[:, -1:])
    grad_inputs = orient(input_back.astype(jnp.bfloat16), mirror)
    cell_count = cycle_rows * col_count
    return (grad_inputs, first_grad / math.sqrt(cell_count), second_grad / math.sqrt(cell_count), third_grad / math.sqrt(cell_count // 4))
```

```python
import math

import jax
import jax.numpy as jnp
from jax import lax
from jax.sharding import PartitionSpec as P


def extended(shard, sides, width):
    for axis, dim in sides:
        devices, length = (lax.axis_size(axis), shard.shape[dim])
        up = [(i, (i + 1) % devices) for i in range(devices)]
        down = [(j, i) for i, j in up]
        last = lax.slice_in_dim(shard, length - width, length, axis=dim)
        leading = lax.slice_in_dim(shard, 0, width, axis=dim)
        before = lax.ppermute(last, axis, up)
        after = lax.ppermute(leading, axis, down)
        shard = jnp.concatenate([before, shard, after], axis=dim)
    return shard


def passed_along(shard, axis, by):
    devices = lax.axis_size(axis)
    return lax.ppermute(shard, axis, [(i, (i + by) % devices) for i in range(devices)])


def orient(block, mirrored):
    return jnp.where(mirrored == 1, block[..., ::-1], block)


def widen(active):
    gathered = lax.all_gather(active, "chan", axis=0, tiled=True)
    return extended(gathered, (("blk", 1),), 1)


def conv_taps(padded, weight):
    row_count = padded.shape[1] - 2
    col_count = padded.shape[2]
    framed = jnp.pad(padded, ((0, 0), (0, 0), (1, 1)))
    running = jnp.zeros((weight.shape[2], row_count, col_count), jnp.float32)
    for row_tap in range(3):
        for col_tap in range(3):
            running = running + jnp.einsum(
                "oi,irw->orw",
                weight[row_tap, col_tap],
                framed[:, row_tap : row_tap + row_count, col_tap : col_tap + col_count],
                preferred_element_type=jnp.float32,
            )
    return running


def weight_taps(grad_out, padded):
    row_count = grad_out.shape[1]
    col_count = grad_out.shape[2]
    framed = jnp.pad(padded, ((0, 0), (0, 0), (1, 1)))
    stacked = []
    for row_tap in range(3):
        line = []
        for col_tap in range(3):
            line.append(
                jnp.einsum(
                    "orw,irw->oi",
                    grad_out,
                    framed[:, row_tap : row_tap + row_count, col_tap : col_tap + col_count],
                    preferred_element_type=jnp.float32,
                )
            )
        stacked.append(jnp.stack(line))
    return jnp.stack(stacked)


def spread_taps(grad_out, weight):
    row_count = grad_out.shape[1]
    col_count = grad_out.shape[2]
    framed = jnp.pad(grad_out, ((0, 0), (2, 2), (2, 2)))
    running = jnp.zeros((weight.shape[3], row_count + 2, col_count), jnp.float32)
    for row_tap in range(3):
        for col_tap in range(3):
            row_start = 2 - row_tap
            col_start = 3 - col_tap
            running = running + jnp.einsum(
                "oi,orw->irw",
                weight[row_tap, col_tap],
                framed[:, row_start : row_start + row_count + 2, col_start : col_start + col_count],
                preferred_element_type=jnp.float32,
            )
    return running


def spread_stride(grad_out, weight):
    out_rows = grad_out.shape[1]
    out_cols = grad_out.shape[2]
    channels = weight.shape[3]
    framed = jnp.pad(grad_out, ((0, 0), (1, 1), (1, 1)))
    parity_rows = []
    for row_par in range(2):
        parity_cols = []
        for col_par in range(2):
            running = jnp.zeros((channels, out_rows + 1, out_cols + 1), jnp.float32)
            for row_tap in range(row_par, 3, 2):
                for col_tap in range(col_par, 3, 2):
                    row_start = 1 - row_tap // 2
                    col_start = 1 - col_tap // 2
                    running = running + jnp.einsum(
                        "oi,orw->irw",
                        weight[row_tap, col_tap],
                        framed[
                            :,
                            row_start : row_start + out_rows + 1,
                            col_start : col_start + out_cols + 1,
                        ],
                        preferred_element_type=jnp.float32,
                    )
            parity_cols.append(running)
        parity_rows.append(jnp.stack(parity_cols, axis=3))
    woven = jnp.stack(parity_rows, axis=2)
    woven = woven.reshape(channels, 2 * out_rows + 2, 2 * out_cols + 2)
    return woven[:, : 2 * out_rows + 1, 1 : 2 * out_cols + 1]


def fold_rims(grad_rows, both_sides):
    interior = grad_rows[:, 1:-1] if both_sides else grad_rows[:, 1:]
    from_next = passed_along(grad_rows[:, :1].astype(jnp.bfloat16), "blk", -1).astype(jnp.float32)
    if both_sides:
        from_prev = passed_along(grad_rows[:, -1:].astype(jnp.bfloat16), "blk", 1).astype(
            jnp.float32
        )
        return jnp.concatenate(
            [interior[:, :1] + from_prev, interior[:, 1:-1], interior[:, -1:] + from_next], axis=1
        )
    return jnp.concatenate([interior[:, :-1], interior[:, -1:] + from_next], axis=1)


def input_grad(delta, weight):
    own_part = lax.psum_scatter(
        spread_taps(delta, weight).astype(jnp.bfloat16), "chan", scatter_dimension=0, tiled=True
    ).astype(jnp.float32)
    return fold_rims(own_part, True)


def third_input_grad(upstream, weight):
    own_part = lax.psum_scatter(
        spread_stride(upstream, weight).astype(jnp.bfloat16),
        "chan",
        scatter_dimension=0,
        tiled=True,
    ).astype(jnp.float32)
    return fold_rims(own_part, False)


def summed_over_cycle(parts, axis):
    devices = lax.axis_size(axis)
    flat = jnp.concatenate([p.reshape(-1) for p in parts])
    pieces = lax.all_to_all(flat.reshape(devices, -1), axis, 0, 0, tiled=True)
    total = jnp.sum(pieces, axis=0)
    spread = jnp.broadcast_to(total[None], (devices,) + total.shape)
    whole = lax.all_to_all(spread, axis, 0, 0, tiled=True).reshape(-1)
    out, start = [], 0
    for p in parts:
        out.append(whole[start : start + p.size].reshape(p.shape))
        start += p.size
    return out


def gelu_back(pre_act, grad_in):
    return jax.vjp(jax.nn.gelu, pre_act)[1](grad_in)[0]


def shards(inputs, w_first, w_second, w_third, cotangent, mirror):
    mirrored = mirror[0]
    oriented = orient(inputs, mirrored)
    upstream = orient(cotangent, mirrored)
    first_pad = widen(oriented)
    first_pre = conv_taps(first_pad, w_first)
    first_act = jax.nn.gelu(first_pre).astype(jnp.bfloat16)
    second_pad = widen(first_act)
    second_pre = conv_taps(second_pad, w_second)
    second_act = jax.nn.gelu(second_pre).astype(jnp.bfloat16)
    second_all = lax.all_gather(second_act, "chan", axis=0, tiled=True)
    wrap_top = passed_along(second_all[:, -1:], "blk", 1)
    framed = jnp.pad(jnp.concatenate([wrap_top, second_all], axis=1), ((0, 0), (0, 0), (1, 0)))
    out_rows = upstream.shape[1]
    out_cols = upstream.shape[2]
    stacked = []
    for row_tap in range(3):
        line = []
        for col_tap in range(3):
            line.append(
                jnp.einsum(
                    "orw,irw->oi",
                    upstream,
                    framed[
                        :,
                        row_tap : row_tap + 2 * out_rows : 2,
                        col_tap : col_tap + 2 * out_cols : 2,
                    ],
                    preferred_element_type=jnp.float32,
                )
            )
        stacked.append(jnp.stack(line))
    third_grad = jnp.stack(stacked)
    second_back = third_input_grad(upstream, w_third)
    second_delta = gelu_back(second_pre, second_back).astype(jnp.bfloat16)
    second_grad = weight_taps(second_delta, second_pad)
    first_back = input_grad(second_delta, w_second)
    first_delta = gelu_back(first_pre, first_back).astype(jnp.bfloat16)
    first_grad = weight_taps(first_delta, first_pad)
    input_back = input_grad(first_delta, w_first).astype(jnp.bfloat16)
    reduced = summed_over_cycle((first_grad, second_grad, third_grad), "blk")
    cell_count = inputs.shape[1] * inputs.shape[2] * lax.axis_size("blk")
    return (
        orient(input_back, mirrored),
        reduced[0] / math.sqrt(cell_count),
        reduced[1] / math.sqrt(cell_count),
        reduced[2] / math.sqrt(cell_count // 4),
    )


def solution(mesh):
    placed = (
        P("chan", "blk", None),
        P(None, None, "chan", None),
        P(None, None, "chan", None),
        P(None, None, "chan", None),
        P("chan", "blk", None),
        P("blk"),
    )
    return jax.shard_map(
        shards,
        mesh=mesh,
        in_specs=placed,
        out_specs=(
            P("chan", "blk", None),
            P(None, None, "chan", None),
            P(None, None, "chan", None),
            P(None, None, "chan", None),
        ),
        check_vma=False,
    )
```

```python
import math

import jax
import jax.numpy as jnp
from jax import lax
from jax.sharding import PartitionSpec as P


def extended(shard, sides, width):
    for axis, dim in sides:
        devices, length = (lax.axis_size(axis), shard.shape[dim])
        up = [(i, (i + 1) % devices) for i in range(devices)]
        down = [(j, i) for i, j in up]
        last = lax.slice_in_dim(shard, length - width, length, axis=dim)
        leading = lax.slice_in_dim(shard, 0, width, axis=dim)
        before = lax.ppermute(last, axis, up)
        after = lax.ppermute(leading, axis, down)
        shard = jnp.concatenate([before, shard, after], axis=dim)
    return shard


def passed_along(shard, axis, by):
    devices = lax.axis_size(axis)
    return lax.ppermute(shard, axis, [(i, (i + by) % devices) for i in range(devices)])


def orient(block, mirrored):
    return jnp.where(mirrored == 1, block[..., ::-1], block)


def widen(active):
    gathered = lax.all_gather(active, "chan", axis=0, tiled=True)
    return extended(gathered, (("blk", 1),), 1)


def conv_taps(padded, weight):
    row_count = padded.shape[1] - 2
    col_count = padded.shape[2]
    framed = jnp.pad(padded, ((0, 0), (0, 0), (1, 1)))
    running = jnp.zeros((weight.shape[2], row_count, col_count), jnp.float32)
    for row_tap in range(3):
        for col_tap in range(3):
            running = running + jnp.einsum(
                "oi,irw->orw",
                weight[row_tap, col_tap],
                framed[:, row_tap : row_tap + row_count, col_tap : col_tap + col_count],
                preferred_element_type=jnp.float32,
            )
    return running


def weight_taps(grad_out, padded):
    row_count = grad_out.shape[1]
    col_count = grad_out.shape[2]
    framed = jnp.pad(padded, ((0, 0), (0, 0), (1, 1)))
    stacked = []
    for row_tap in range(3):
        line = []
        for col_tap in range(3):
            line.append(
                jnp.einsum(
                    "orw,irw->oi",
                    grad_out,
                    framed[:, row_tap : row_tap + row_count, col_tap : col_tap + col_count],
                    preferred_element_type=jnp.float32,
                )
            )
        stacked.append(jnp.stack(line))
    return jnp.stack(stacked)


def spread_taps(grad_out, weight):
    row_count = grad_out.shape[1]
    col_count = grad_out.shape[2]
    framed = jnp.pad(grad_out, ((0, 0), (2, 2), (2, 2)))
    running = jnp.zeros((weight.shape[3], row_count + 2, col_count), jnp.float32)
    for row_tap in range(3):
        for col_tap in range(3):
            row_start = 2 - row_tap
            col_start = 3 - col_tap
            running = running + jnp.einsum(
                "oi,orw->irw",
                weight[row_tap, col_tap],
                framed[:, row_start : row_start + row_count + 2, col_start : col_start + col_count],
                preferred_element_type=jnp.float32,
            )
    return running


def spread_stride(grad_out, weight):
    out_rows = grad_out.shape[1]
    out_cols = grad_out.shape[2]
    channels = weight.shape[3]
    framed = jnp.pad(grad_out, ((0, 0), (1, 1), (1, 1)))
    parity_rows = []
    for row_par in range(2):
        parity_cols = []
        for col_par in range(2):
            running = jnp.zeros((channels, out_rows + 1, out_cols + 1), jnp.float32)
            for row_tap in range(row_par, 3, 2):
                for col_tap in range(col_par, 3, 2):
                    row_start = 1 - row_tap // 2
                    col_start = 1 - col_tap // 2
                    running = running + jnp.einsum(
                        "oi,orw->irw",
                        weight[row_tap, col_tap],
                        framed[
                            :,
                            row_start : row_start + out_rows + 1,
                            col_start : col_start + out_cols + 1,
                        ],
                        preferred_element_type=jnp.float32,
                    )
            parity_cols.append(running)
        parity_rows.append(jnp.stack(parity_cols, axis=3))
    woven = jnp.stack(parity_rows, axis=2)
    woven = woven.reshape(channels, 2 * out_rows + 2, 2 * out_cols + 2)
    return woven[:, : 2 * out_rows + 1, 1 : 2 * out_cols + 1]


def fold_rims(grad_rows, both_sides):
    interior = grad_rows[:, 1:-1] if both_sides else grad_rows[:, 1:]
    from_next = passed_along(grad_rows[:, :1].astype(jnp.bfloat16), "blk", -1).astype(jnp.float32)
    if both_sides:
        from_prev = passed_along(grad_rows[:, -1:].astype(jnp.bfloat16), "blk", 1).astype(
            jnp.float32
        )
        return jnp.concatenate(
            [interior[:, :1] + from_prev, interior[:, 1:-1], interior[:, -1:] + from_next], axis=1
        )
    return jnp.concatenate([interior[:, :-1], interior[:, -1:] + from_next], axis=1)


def input_grad(delta, weight):
    own_part = lax.psum_scatter(
        spread_taps(delta, weight).astype(jnp.bfloat16), "chan", scatter_dimension=0, tiled=True
    ).astype(jnp.float32)
    return fold_rims(own_part, True)


def third_input_grad(upstream, weight):
    own_part = lax.psum_scatter(
        spread_stride(upstream, weight).astype(jnp.bfloat16),
        "chan",
        scatter_dimension=0,
        tiled=True,
    ).astype(jnp.float32)
    return fold_rims(own_part, False)


def parity_picker(cols, out_cols):
    source = lax.broadcasted_iota(jnp.int32, (cols, 3 * out_cols), 0)
    target = lax.broadcasted_iota(jnp.int32, (cols, 3 * out_cols), 1)
    wanted = 2 * (target % out_cols) + target // out_cols - 1
    return (source == wanted).astype(jnp.bfloat16)


def summed_over_cycle(parts, axis):
    devices = lax.axis_size(axis)
    flat = jnp.concatenate([p.reshape(-1) for p in parts])
    pieces = lax.all_to_all(flat.reshape(devices, -1), axis, 0, 0, tiled=True)
    total = jnp.sum(pieces, axis=0)
    spread = jnp.broadcast_to(total[None], (devices,) + total.shape)
    whole = lax.all_to_all(spread, axis, 0, 0, tiled=True).reshape(-1)
    out, start = [], 0
    for p in parts:
        out.append(whole[start : start + p.size].reshape(p.shape))
        start += p.size
    return out


def gelu_back(pre_act, grad_in):
    return jax.vjp(jax.nn.gelu, pre_act)[1](grad_in)[0]


def shards(inputs, w_first, w_second, w_third, cotangent, mirror):
    mirrored = mirror[0]
    oriented = orient(inputs, mirrored)
    upstream = orient(cotangent, mirrored)
    first_pad = widen(oriented)
    first_pre = conv_taps(first_pad, w_first)
    first_act = jax.nn.gelu(first_pre).astype(jnp.bfloat16)
    second_pad = widen(first_act)
    second_pre = conv_taps(second_pad, w_second)
    second_act = jax.nn.gelu(second_pre).astype(jnp.bfloat16)
    second_all = lax.all_gather(second_act, "chan", axis=0, tiled=True)
    wrap_top = passed_along(second_all[:, -1:], "blk", 1)
    stride_rows = jnp.concatenate([wrap_top, second_all], axis=1)
    out_rows = upstream.shape[1]
    out_cols = upstream.shape[2]
    by_parity = jnp.einsum(
        "irt,tk->irk",
        stride_rows,
        parity_picker(2 * out_cols, out_cols),
        preferred_element_type=jnp.float32,
    ).astype(jnp.bfloat16)
    stacked = []
    for row_tap in range(3):
        line = []
        for col_tap in range(3):
            line.append(
                jnp.einsum(
                    "orw,irw->oi",
                    upstream,
                    by_parity[
                        :,
                        row_tap : row_tap + 2 * out_rows : 2,
                        col_tap * out_cols : (col_tap + 1) * out_cols,
                    ],
                    preferred_element_type=jnp.float32,
                )
            )
        stacked.append(jnp.stack(line))
    third_grad = jnp.stack(stacked)
    (third_grad,) = summed_over_cycle((third_grad,), "blk")
    second_back = third_input_grad(upstream, w_third)
    second_delta = gelu_back(second_pre, second_back).astype(jnp.bfloat16)
    second_grad = weight_taps(second_delta, second_pad)
    first_back = input_grad(second_delta, w_second)
    first_delta = gelu_back(first_pre, first_back).astype(jnp.bfloat16)
    first_grad = weight_taps(first_delta, first_pad)
    input_back = input_grad(first_delta, w_first).astype(jnp.bfloat16)
    reduced = summed_over_cycle((first_grad, second_grad), "blk") + [third_grad]
    cell_count = inputs.shape[1] * inputs.shape[2] * lax.axis_size("blk")
    return (
        orient(input_back, mirrored),
        reduced[0] / math.sqrt(cell_count),
        reduced[1] / math.sqrt(cell_count),
        reduced[2] / math.sqrt(cell_count // 4),
    )


def solution(mesh):
    placed = (
        P("chan", "blk", None),
        P(None, None, "chan", None),
        P(None, None, "chan", None),
        P(None, None, "chan", None),
        P("chan", "blk", None),
        P("blk"),
    )
    return jax.shard_map(
        shards,
        mesh=mesh,
        in_specs=placed,
        out_specs=(
            P("chan", "blk", None),
            P(None, None, "chan", None),
            P(None, None, "chan", None),
            P(None, None, "chan", None),
        ),
        check_vma=False,
    )
```

```python
import math

import jax
import jax.numpy as jnp
from jax import lax
from jax.sharding import PartitionSpec as P


def extended(shard, sides, width):
    for axis, dim in sides:
        devices, length = (lax.axis_size(axis), shard.shape[dim])
        up = [(i, (i + 1) % devices) for i in range(devices)]
        down = [(j, i) for i, j in up]
        last = lax.slice_in_dim(shard, length - width, length, axis=dim)
        leading = lax.slice_in_dim(shard, 0, width, axis=dim)
        before = lax.ppermute(last, axis, up)
        after = lax.ppermute(leading, axis, down)
        shard = jnp.concatenate([before, shard, after], axis=dim)
    return shard


def passed_along(shard, axis, by):
    devices = lax.axis_size(axis)
    return lax.ppermute(shard, axis, [(i, (i + by) % devices) for i in range(devices)])


def orient(block, mirrored):
    return jnp.where(mirrored == 1, block[..., ::-1], block)


def widen(active):
    gathered = lax.all_gather(active, "chan", axis=0, tiled=True)
    return extended(gathered, (("blk", 1),), 1)


def conv_taps(padded, weight):
    row_count = padded.shape[1] - 2
    col_count = padded.shape[2]
    framed = jnp.pad(padded, ((0, 0), (0, 0), (1, 1)))
    running = jnp.zeros((weight.shape[2], row_count, col_count), jnp.float32)
    for row_tap in range(3):
        for col_tap in range(3):
            running = running + jnp.einsum(
                "oi,irw->orw",
                weight[row_tap, col_tap],
                framed[:, row_tap : row_tap + row_count, col_tap : col_tap + col_count],
                preferred_element_type=jnp.float32,
            )
    return running


def weight_taps(grad_out, padded):
    row_count = grad_out.shape[1]
    col_count = grad_out.shape[2]
    framed = jnp.pad(padded, ((0, 0), (0, 0), (1, 1)))
    stacked = []
    for row_tap in range(3):
        line = []
        for col_tap in range(3):
            line.append(
                jnp.einsum(
                    "orw,irw->oi",
                    grad_out,
                    framed[:, row_tap : row_tap + row_count, col_tap : col_tap + col_count],
                    preferred_element_type=jnp.float32,
                )
            )
        stacked.append(jnp.stack(line))
    return jnp.stack(stacked)


def spread_taps(grad_out, weight):
    row_count = grad_out.shape[1]
    col_count = grad_out.shape[2]
    framed = jnp.pad(grad_out, ((0, 0), (2, 2), (2, 2)))
    running = jnp.zeros((weight.shape[3], row_count + 2, col_count), jnp.float32)
    for row_tap in range(3):
        for col_tap in range(3):
            row_start = 2 - row_tap
            col_start = 3 - col_tap
            running = running + jnp.einsum(
                "oi,orw->irw",
                weight[row_tap, col_tap],
                framed[:, row_start : row_start + row_count + 2, col_start : col_start + col_count],
                preferred_element_type=jnp.float32,
            )
    return running


def spread_stride(grad_out, weight):
    out_rows = grad_out.shape[1]
    out_cols = grad_out.shape[2]
    channels = weight.shape[3]
    framed = jnp.pad(grad_out, ((0, 0), (1, 1), (1, 1)))
    parity_rows = []
    for row_par in range(2):
        parity_cols = []
        for col_par in range(2):
            running = jnp.zeros((channels, out_rows + 1, out_cols + 1), jnp.float32)
            for row_tap in range(row_par, 3, 2):
                for col_tap in range(col_par, 3, 2):
                    row_start = 1 - row_tap // 2
                    col_start = 1 - col_tap // 2
                    running = running + jnp.einsum(
                        "oi,orw->irw",
                        weight[row_tap, col_tap],
                        framed[
                            :,
                            row_start : row_start + out_rows + 1,
                            col_start : col_start + out_cols + 1,
                        ],
                        preferred_element_type=jnp.float32,
                    )
            parity_cols.append(running)
        parity_rows.append(jnp.stack(parity_cols, axis=3))
    woven = jnp.stack(parity_rows, axis=2)
    woven = woven.reshape(channels, 2 * out_rows + 2, 2 * out_cols + 2)
    return woven[:, : 2 * out_rows + 1, 1 : 2 * out_cols + 1]


def fold_rims(grad_rows, both_sides):
    interior = grad_rows[:, 1:-1] if both_sides else grad_rows[:, 1:]
    from_next = passed_along(grad_rows[:, :1].astype(jnp.bfloat16), "blk", -1).astype(jnp.float32)
    if both_sides:
        from_prev = passed_along(grad_rows[:, -1:].astype(jnp.bfloat16), "blk", 1).astype(
            jnp.float32
        )
        return jnp.concatenate(
            [interior[:, :1] + from_prev, interior[:, 1:-1], interior[:, -1:] + from_next], axis=1
        )
    return jnp.concatenate([interior[:, :-1], interior[:, -1:] + from_next], axis=1)


def input_grad(delta, weight):
    own_part = lax.psum_scatter(
        spread_taps(delta, weight).astype(jnp.bfloat16), "chan", scatter_dimension=0, tiled=True
    ).astype(jnp.float32)
    return fold_rims(own_part, True)


def third_input_grad(upstream, weight):
    own_part = lax.psum_scatter(
        spread_stride(upstream, weight).astype(jnp.bfloat16),
        "chan",
        scatter_dimension=0,
        tiled=True,
    ).astype(jnp.float32)
    return fold_rims(own_part, False)


def parity_picker(cols, out_cols):
    source = lax.broadcasted_iota(jnp.int32, (cols, 3 * out_cols), 0)
    target = lax.broadcasted_iota(jnp.int32, (cols, 3 * out_cols), 1)
    wanted = 2 * (target % out_cols) + target // out_cols - 1
    return (source == wanted).astype(jnp.bfloat16)


def summed_over_cycle(parts, axis):
    devices = lax.axis_size(axis)
    flat = jnp.concatenate([p.reshape(-1) for p in parts])
    pieces = lax.all_to_all(flat.reshape(devices, -1), axis, 0, 0, tiled=True)
    total = jnp.sum(pieces, axis=0)
    spread = jnp.broadcast_to(total[None], (devices,) + total.shape)
    whole = lax.all_to_all(spread, axis, 0, 0, tiled=True).reshape(-1)
    out, start = [], 0
    for p in parts:
        out.append(whole[start : start + p.size].reshape(p.shape))
        start += p.size
    return out


def gelu_back(pre_act, grad_in):
    return jax.vjp(jax.nn.gelu, pre_act)[1](grad_in)[0]


def shards(inputs, w_first, w_second, w_third, cotangent, mirror):
    mirrored = mirror[0]
    oriented = orient(inputs, mirrored)
    upstream = orient(cotangent, mirrored)
    first_pad = widen(oriented)
    first_pre = conv_taps(first_pad, w_first)
    first_act = jax.nn.gelu(first_pre).astype(jnp.bfloat16)
    second_pad = widen(first_act)
    second_pre = conv_taps(second_pad, w_second)
    second_act = jax.nn.gelu(second_pre).astype(jnp.bfloat16)
    second_all = lax.all_gather(second_act, "chan", axis=0, tiled=True)
    wrap_top = passed_along(second_all[:, -1:], "blk", 1)
    stride_rows = jnp.concatenate([wrap_top, second_all], axis=1)
    out_rows = upstream.shape[1]
    out_cols = upstream.shape[2]
    by_parity = jnp.einsum(
        "irt,tk->irk",
        stride_rows,
        parity_picker(2 * out_cols, out_cols),
        preferred_element_type=jnp.float32,
    ).astype(jnp.bfloat16)
    spaced = jnp.stack([upstream, jnp.zeros_like(upstream)], axis=2).reshape(
        upstream.shape[0], 2 * out_rows, out_cols
    )
    row_placed = jnp.stack(
        [jnp.pad(spaced, ((0, 0), (row_tap, 1), (0, 0)))[:, : 2 * out_rows + 1] for row_tap in range(3)]
    )
    third_grad = jnp.stack(
        [
            jnp.einsum(
                "aosc,isc->aoi",
                row_placed,
                by_parity[:, :, col_tap * out_cols : (col_tap + 1) * out_cols],
                preferred_element_type=jnp.float32,
            )
            for col_tap in range(3)
        ],
        axis=1,
    )
    second_back = third_input_grad(upstream, w_third)
    second_delta = gelu_back(second_pre, second_back).astype(jnp.bfloat16)
    second_grad = weight_taps(second_delta, second_pad)
    first_back = input_grad(second_delta, w_second)
    first_delta = gelu_back(first_pre, first_back).astype(jnp.bfloat16)
    first_grad = weight_taps(first_delta, first_pad)
    input_back = input_grad(first_delta, w_first).astype(jnp.bfloat16)
    reduced = summed_over_cycle((first_grad, second_grad, third_grad), "blk")
    cell_count = inputs.shape[1] * inputs.shape[2] * lax.axis_size("blk")
    return (
        orient(input_back, mirrored),
        reduced[0] / math.sqrt(cell_count),
        reduced[1] / math.sqrt(cell_count),
        reduced[2] / math.sqrt(cell_count // 4),
    )


def solution(mesh):
    placed = (
        P("chan", "blk", None),
        P(None, None, "chan", None),
        P(None, None, "chan", None),
        P(None, None, "chan", None),
        P("chan", "blk", None),
        P("blk"),
    )
    return jax.shard_map(
        shards,
        mesh=mesh,
        in_specs=placed,
        out_specs=(
            P("chan", "blk", None),
            P(None, None, "chan", None),
            P(None, None, "chan", None),
            P(None, None, "chan", None),
        ),
        check_vma=False,
    )
```

```python
import math

import jax
import jax.numpy as jnp
from jax import lax
from jax.sharding import PartitionSpec as P


def extended(shard, sides, width):
    for axis, dim in sides:
        devices, length = (lax.axis_size(axis), shard.shape[dim])
        up = [(i, (i + 1) % devices) for i in range(devices)]
        down = [(j, i) for i, j in up]
        last = lax.slice_in_dim(shard, length - width, length, axis=dim)
        leading = lax.slice_in_dim(shard, 0, width, axis=dim)
        before = lax.ppermute(last, axis, up)
        after = lax.ppermute(leading, axis, down)
        shard = jnp.concatenate([before, shard, after], axis=dim)
    return shard


def passed_along(shard, axis, by):
    devices = lax.axis_size(axis)
    return lax.ppermute(shard, axis, [(i, (i + by) % devices) for i in range(devices)])


def orient(block, mirrored):
    return jnp.where(mirrored == 1, block[..., ::-1], block)


def widen(active):
    gathered = lax.all_gather(active, "chan", axis=0, tiled=True)
    return extended(gathered, (("blk", 1),), 1)


def conv_taps(padded, weight):
    row_count = padded.shape[1] - 2
    col_count = padded.shape[2]
    framed = jnp.pad(padded, ((0, 0), (0, 0), (1, 1)))
    running = jnp.zeros((weight.shape[2], row_count, col_count), jnp.float32)
    for row_tap in range(3):
        for col_tap in range(3):
            running = running + jnp.einsum(
                "oi,irw->orw",
                weight[row_tap, col_tap],
                framed[:, row_tap : row_tap + row_count, col_tap : col_tap + col_count],
                preferred_element_type=jnp.float32,
            )
    return running


def weight_taps(grad_out, padded):
    row_count = grad_out.shape[1]
    col_count = grad_out.shape[2]
    framed = jnp.pad(padded, ((0, 0), (0, 0), (1, 1)))
    stacked = []
    for row_tap in range(3):
        line = []
        for col_tap in range(3):
            line.append(
                jnp.einsum(
                    "orw,irw->oi",
                    grad_out,
                    framed[:, row_tap : row_tap + row_count, col_tap : col_tap + col_count],
                    preferred_element_type=jnp.float32,
                )
            )
        stacked.append(jnp.stack(line))
    return jnp.stack(stacked)


def spread_taps(grad_out, weight):
    row_count = grad_out.shape[1]
    col_count = grad_out.shape[2]
    framed = jnp.pad(grad_out, ((0, 0), (2, 2), (2, 2)))
    running = jnp.zeros((weight.shape[3], row_count + 2, col_count), jnp.float32)
    for row_tap in range(3):
        for col_tap in range(3):
            row_start = 2 - row_tap
            col_start = 3 - col_tap
            running = running + jnp.einsum(
                "oi,orw->irw",
                weight[row_tap, col_tap],
                framed[:, row_start : row_start + row_count + 2, col_start : col_start + col_count],
                preferred_element_type=jnp.float32,
            )
    return running


def spread_stride(grad_out, weight):
    out_rows = grad_out.shape[1]
    out_cols = grad_out.shape[2]
    channels = weight.shape[3]
    framed = jnp.pad(grad_out, ((0, 0), (1, 1), (1, 1)))
    parity_rows = []
    for row_par in range(2):
        parity_cols = []
        for col_par in range(2):
            running = jnp.zeros((channels, out_rows + 1, out_cols + 1), jnp.float32)
            for row_tap in range(row_par, 3, 2):
                for col_tap in range(col_par, 3, 2):
                    row_start = 1 - row_tap // 2
                    col_start = 1 - col_tap // 2
                    running = running + jnp.einsum(
                        "oi,orw->irw",
                        weight[row_tap, col_tap],
                        framed[
                            :,
                            row_start : row_start + out_rows + 1,
                            col_start : col_start + out_cols + 1,
                        ],
                        preferred_element_type=jnp.float32,
                    )
            parity_cols.append(running)
        parity_rows.append(jnp.stack(parity_cols, axis=3))
    woven = jnp.stack(parity_rows, axis=2)
    woven = woven.reshape(channels, 2 * out_rows + 2, 2 * out_cols + 2)
    return woven[:, : 2 * out_rows + 1, 1 : 2 * out_cols + 1]


def fold_rims(grad_rows, both_sides):
    interior = grad_rows[:, 1:-1] if both_sides else grad_rows[:, 1:]
    from_next = passed_along(grad_rows[:, :1].astype(jnp.bfloat16), "blk", -1).astype(jnp.float32)
    if both_sides:
        from_prev = passed_along(grad_rows[:, -1:].astype(jnp.bfloat16), "blk", 1).astype(
            jnp.float32
        )
        return jnp.concatenate(
            [interior[:, :1] + from_prev, interior[:, 1:-1], interior[:, -1:] + from_next], axis=1
        )
    return jnp.concatenate([interior[:, :-1], interior[:, -1:] + from_next], axis=1)


def own_inputs(weight):
    whole = lax.all_gather(weight, "chan", axis=2, tiled=True)
    width = whole.shape[3] // lax.axis_size("chan")
    return lax.dynamic_slice_in_dim(whole, lax.axis_index("chan") * width, width, axis=3)


def input_grad(delta, weight):
    every = lax.all_gather(delta, "chan", axis=0, tiled=True)
    return fold_rims(spread_taps(every, weight), True)


def third_input_grad(upstream, weight):
    every = lax.all_gather(upstream, "chan", axis=0, tiled=True)
    return fold_rims(spread_stride(every, weight), False)


def parity_picker(cols, out_cols):
    source = lax.broadcasted_iota(jnp.int32, (cols, 3 * out_cols), 0)
    target = lax.broadcasted_iota(jnp.int32, (cols, 3 * out_cols), 1)
    wanted = 2 * (target % out_cols) + target // out_cols - 1
    return (source == wanted).astype(jnp.bfloat16)


def summed_over_cycle(parts, axis):
    devices = lax.axis_size(axis)
    flat = jnp.concatenate([p.reshape(-1) for p in parts])
    pieces = lax.all_to_all(flat.reshape(devices, -1), axis, 0, 0, tiled=True)
    total = jnp.sum(pieces, axis=0)
    spread = jnp.broadcast_to(total[None], (devices,) + total.shape)
    whole = lax.all_to_all(spread, axis, 0, 0, tiled=True).reshape(-1)
    out, start = [], 0
    for p in parts:
        out.append(whole[start : start + p.size].reshape(p.shape))
        start += p.size
    return out


def gelu_back(pre_act, grad_in):
    return jax.vjp(jax.nn.gelu, pre_act)[1](grad_in)[0]


def shards(inputs, w_first, w_second, w_third, cotangent, mirror):
    mirrored = mirror[0]
    oriented = orient(inputs, mirrored)
    upstream = orient(cotangent, mirrored)
    first_pad = widen(oriented)
    first_pre = conv_taps(first_pad, w_first)
    first_act = jax.nn.gelu(first_pre).astype(jnp.bfloat16)
    second_pad = widen(first_act)
    second_pre = conv_taps(second_pad, w_second)
    second_act = jax.nn.gelu(second_pre).astype(jnp.bfloat16)
    second_all = lax.all_gather(second_act, "chan", axis=0, tiled=True)
    wrap_top = passed_along(second_all[:, -1:], "blk", 1)
    stride_rows = jnp.concatenate([wrap_top, second_all], axis=1)
    out_rows = upstream.shape[1]
    out_cols = upstream.shape[2]
    by_parity = jnp.einsum(
        "irt,tk->irk",
        stride_rows,
        parity_picker(2 * out_cols, out_cols),
        preferred_element_type=jnp.float32,
    ).astype(jnp.bfloat16)
    spaced = jnp.stack([upstream, jnp.zeros_like(upstream)], axis=2).reshape(
        upstream.shape[0], 2 * out_rows, out_cols
    )
    row_placed = jnp.stack(
        [jnp.pad(spaced, ((0, 0), (row_tap, 1), (0, 0)))[:, : 2 * out_rows + 1] for row_tap in range(3)]
    )
    third_grad = jnp.stack(
        [
            jnp.einsum(
                "aosc,isc->aoi",
                row_placed,
                by_parity[:, :, col_tap * out_cols : (col_tap + 1) * out_cols],
                preferred_element_type=jnp.float32,
            )
            for col_tap in range(3)
        ],
        axis=1,
    )
    second_back = third_input_grad(upstream, own_inputs(w_third))
    second_delta = gelu_back(second_pre, second_back).astype(jnp.bfloat16)
    second_grad = weight_taps(second_delta, second_pad)
    first_back = input_grad(second_delta, own_inputs(w_second))
    first_delta = gelu_back(first_pre, first_back).astype(jnp.bfloat16)
    first_grad = weight_taps(first_delta, first_pad)
    input_back = input_grad(first_delta, own_inputs(w_first)).astype(jnp.bfloat16)
    reduced = summed_over_cycle((first_grad, second_grad, third_grad), "blk")
    cell_count = inputs.shape[1] * inputs.shape[2] * lax.axis_size("blk")
    return (
        orient(input_back, mirrored),
        reduced[0] / math.sqrt(cell_count),
        reduced[1] / math.sqrt(cell_count),
        reduced[2] / math.sqrt(cell_count // 4),
    )


def solution(mesh):
    placed = (
        P("chan", "blk", None),
        P(None, None, "chan", None),
        P(None, None, "chan", None),
        P(None, None, "chan", None),
        P("chan", "blk", None),
        P("blk"),
    )
    return jax.shard_map(
        shards,
        mesh=mesh,
        in_specs=placed,
        out_specs=(
            P("chan", "blk", None),
            P(None, None, "chan", None),
            P(None, None, "chan", None),
            P(None, None, "chan", None),
        ),
        check_vma=False,
    )
```

```python
import math

import jax
import jax.numpy as jnp
from jax import lax
from jax.sharding import PartitionSpec as P


def extended(shard, sides, width):
    for axis, dim in sides:
        devices, length = (lax.axis_size(axis), shard.shape[dim])
        up = [(i, (i + 1) % devices) for i in range(devices)]
        down = [(j, i) for i, j in up]
        last = lax.slice_in_dim(shard, length - width, length, axis=dim)
        leading = lax.slice_in_dim(shard, 0, width, axis=dim)
        before = lax.ppermute(last, axis, up)
        after = lax.ppermute(leading, axis, down)
        shard = jnp.concatenate([before, shard, after], axis=dim)
    return shard


def passed_along(shard, axis, by):
    devices = lax.axis_size(axis)
    return lax.ppermute(shard, axis, [(i, (i + by) % devices) for i in range(devices)])


def orient(block, mirrored):
    return jnp.where(mirrored == 1, block[..., ::-1], block)


def widen(active):
    gathered = lax.all_gather(active, "chan", axis=0, tiled=True)
    return extended(gathered, (("blk", 1),), 1)


def conv_taps(padded, weight):
    row_count = padded.shape[1] - 2
    col_count = padded.shape[2]
    framed = jnp.pad(padded, ((0, 0), (0, 0), (1, 1)))
    running = jnp.zeros((weight.shape[2], row_count, col_count), jnp.float32)
    for row_tap in range(3):
        for col_tap in range(3):
            running = running + jnp.einsum(
                "oi,irw->orw",
                weight[row_tap, col_tap],
                framed[:, row_tap : row_tap + row_count, col_tap : col_tap + col_count],
                preferred_element_type=jnp.float32,
            )
    return running


def weight_taps(grad_out, padded):
    row_count = grad_out.shape[1]
    col_count = grad_out.shape[2]
    framed = jnp.pad(padded, ((0, 0), (0, 0), (1, 1)))
    stacked = []
    for row_tap in range(3):
        line = []
        for col_tap in range(3):
            line.append(
                jnp.einsum(
                    "orw,irw->oi",
                    grad_out,
                    framed[:, row_tap : row_tap + row_count, col_tap : col_tap + col_count],
                    preferred_element_type=jnp.float32,
                )
            )
        stacked.append(jnp.stack(line))
    return jnp.stack(stacked)


def spread_taps(grad_out, weight):
    row_count = grad_out.shape[1]
    col_count = grad_out.shape[2]
    framed = jnp.pad(grad_out, ((0, 0), (2, 2), (2, 2)))
    running = jnp.zeros((weight.shape[3], row_count + 2, col_count), jnp.float32)
    for row_tap in range(3):
        for col_tap in range(3):
            row_start = 2 - row_tap
            col_start = 3 - col_tap
            running = running + jnp.einsum(
                "oi,orw->irw",
                weight[row_tap, col_tap],
                framed[:, row_start : row_start + row_count + 2, col_start : col_start + col_count],
                preferred_element_type=jnp.float32,
            )
    return running


def spread_stride(grad_out, weight):
    out_rows = grad_out.shape[1]
    out_cols = grad_out.shape[2]
    channels = weight.shape[3]
    framed = jnp.pad(grad_out, ((0, 0), (1, 1), (1, 1)))
    parity_rows = []
    for row_par in range(2):
        parity_cols = []
        for col_par in range(2):
            running = jnp.zeros((channels, out_rows + 1, out_cols + 1), jnp.float32)
            for row_tap in range(row_par, 3, 2):
                for col_tap in range(col_par, 3, 2):
                    row_start = 1 - row_tap // 2
                    col_start = 1 - col_tap // 2
                    running = running + jnp.einsum(
                        "oi,orw->irw",
                        weight[row_tap, col_tap],
                        framed[
                            :,
                            row_start : row_start + out_rows + 1,
                            col_start : col_start + out_cols + 1,
                        ],
                        preferred_element_type=jnp.float32,
                    )
            parity_cols.append(running)
        parity_rows.append(jnp.stack(parity_cols, axis=3))
    woven = jnp.stack(parity_rows, axis=2)
    woven = woven.reshape(channels, 2 * out_rows + 2, 2 * out_cols + 2)
    return woven[:, : 2 * out_rows + 1, 1 : 2 * out_cols + 1]


def fold_rims(grad_rows, both_sides):
    interior = grad_rows[:, 1:-1] if both_sides else grad_rows[:, 1:]
    from_next = passed_along(grad_rows[:, :1].astype(jnp.bfloat16), "blk", -1).astype(jnp.float32)
    if both_sides:
        from_prev = passed_along(grad_rows[:, -1:].astype(jnp.bfloat16), "blk", 1).astype(
            jnp.float32
        )
        return jnp.concatenate(
            [interior[:, :1] + from_prev, interior[:, 1:-1], interior[:, -1:] + from_next], axis=1
        )
    return jnp.concatenate([interior[:, :-1], interior[:, -1:] + from_next], axis=1)


def own_inputs(weight):
    whole = lax.all_gather(weight, "chan", axis=2, tiled=True)
    width = whole.shape[3] // lax.axis_size("chan")
    return lax.dynamic_slice_in_dim(whole, lax.axis_index("chan") * width, width, axis=3)


def input_grad(delta, weight):
    every = lax.all_gather(delta, "chan", axis=0, tiled=True)
    return fold_rims(spread_taps(every, weight), True)


def third_input_grad(upstream, weight):
    every = lax.all_gather(upstream, "chan", axis=0, tiled=True)
    return fold_rims(spread_stride(every, weight), False)


def parity_picker(cols, out_cols):
    source = lax.broadcasted_iota(jnp.int32, (cols, 3 * out_cols), 0)
    target = lax.broadcasted_iota(jnp.int32, (cols, 3 * out_cols), 1)
    wanted = 2 * (target % out_cols) + target // out_cols - 1
    return (source == wanted).astype(jnp.bfloat16)


def summed_over_cycle(parts, axis):
    devices = lax.axis_size(axis)
    flat = jnp.concatenate([p.reshape(-1) for p in parts])
    pieces = lax.all_to_all(flat.reshape(devices, -1), axis, 0, 0, tiled=True)
    total = jnp.sum(pieces, axis=0)
    spread = jnp.broadcast_to(total[None], (devices,) + total.shape)
    whole = lax.all_to_all(spread, axis, 0, 0, tiled=True).reshape(-1)
    out, start = [], 0
    for p in parts:
        out.append(whole[start : start + p.size].reshape(p.shape))
        start += p.size
    return out


def gelu_back(pre_act, grad_in):
    return jax.vjp(jax.nn.gelu, pre_act)[1](grad_in)[0]


def shards(inputs, w_first, w_second, w_third, cotangent, mirror):
    mirrored = mirror[0]
    oriented = orient(inputs, mirrored)
    upstream = orient(cotangent, mirrored)
    first_pad = widen(oriented)
    first_pre = conv_taps(first_pad, w_first)
    first_act = jax.nn.gelu(first_pre).astype(jnp.bfloat16)
    second_pad = widen(first_act)
    second_pre = conv_taps(second_pad, w_second)
    second_act = jax.nn.gelu(second_pre).astype(jnp.bfloat16)
    second_all = lax.all_gather(second_act, "chan", axis=0, tiled=True)
    wrap_top = passed_along(second_all[:, -1:], "blk", 1)
    stride_rows = jnp.concatenate([wrap_top, second_all], axis=1)
    out_rows = upstream.shape[1]
    out_cols = upstream.shape[2]
    by_parity = jnp.einsum(
        "irt,tk->irk",
        stride_rows,
        parity_picker(2 * out_cols, out_cols),
        preferred_element_type=jnp.float32,
    ).astype(jnp.bfloat16)
    spaced = jnp.stack([upstream, jnp.zeros_like(upstream)], axis=2).reshape(
        upstream.shape[0], 2 * out_rows, out_cols
    )
    row_placed = jnp.stack(
        [jnp.pad(spaced, ((0, 0), (row_tap, 1), (0, 0)))[:, : 2 * out_rows + 1] for row_tap in range(3)]
    )
    third_grad = jnp.stack(
        [
            jnp.einsum(
                "aosc,isc->aoi",
                row_placed,
                by_parity[:, :, col_tap * out_cols : (col_tap + 1) * out_cols],
                preferred_element_type=jnp.float32,
            )
            for col_tap in range(3)
        ],
        axis=1,
    )
    second_back = third_input_grad(upstream, own_inputs(w_third))
    second_delta = gelu_back(second_pre, second_back).astype(jnp.bfloat16)
    second_grad = weight_taps(second_delta, second_pad)
    first_back = input_grad(second_delta, own_inputs(w_second))
    first_delta = gelu_back(first_pre, first_back).astype(jnp.bfloat16)
    first_grad = weight_taps(first_delta, first_pad)
    input_back = input_grad(first_delta, own_inputs(w_first)).astype(jnp.bfloat16)
    input_back, grads = lax.optimization_barrier((input_back, (first_grad, second_grad, third_grad)))
    reduced = summed_over_cycle(grads, "blk")
    cell_count = inputs.shape[1] * inputs.shape[2] * lax.axis_size("blk")
    return (
        orient(input_back, mirrored),
        reduced[0] / math.sqrt(cell_count),
        reduced[1] / math.sqrt(cell_count),
        reduced[2] / math.sqrt(cell_count // 4),
    )


def solution(mesh):
    placed = (
        P("chan", "blk", None),
        P(None, None, "chan", None),
        P(None, None, "chan", None),
        P(None, None, "chan", None),
        P("chan", "blk", None),
        P("blk"),
    )
    return jax.shard_map(
        shards,
        mesh=mesh,
        in_specs=placed,
        out_specs=(
            P("chan", "blk", None),
            P(None, None, "chan", None),
            P(None, None, "chan", None),
            P(None, None, "chan", None),
        ),
        check_vma=False,
    )
```

```python
import math

import jax
import jax.numpy as jnp
from jax import lax
from jax.sharding import PartitionSpec as P


def extended(shard, sides, width):
    for axis, dim in sides:
        devices, length = (lax.axis_size(axis), shard.shape[dim])
        up = [(i, (i + 1) % devices) for i in range(devices)]
        down = [(j, i) for i, j in up]
        last = lax.slice_in_dim(shard, length - width, length, axis=dim)
        leading = lax.slice_in_dim(shard, 0, width, axis=dim)
        before = lax.ppermute(last, axis, up)
        after = lax.ppermute(leading, axis, down)
        shard = jnp.concatenate([before, shard, after], axis=dim)
    return shard


def passed_along(shard, axis, by):
    devices = lax.axis_size(axis)
    return lax.ppermute(shard, axis, [(i, (i + by) % devices) for i in range(devices)])


def orient(block, mirrored):
    return jnp.where(mirrored == 1, block[..., ::-1], block)


def widen(active):
    gathered = lax.all_gather(active, "chan", axis=0, tiled=True)
    return extended(gathered, (("blk", 1),), 1)


def widen_by(active, before_rows, after_rows):
    gathered = lax.all_gather(active, "chan", axis=0, tiled=True)
    devices, length = lax.axis_size("blk"), gathered.shape[1]
    up = [(i, (i + 1) % devices) for i in range(devices)]
    down = [(j, i) for i, j in up]
    before = lax.ppermute(gathered[:, length - before_rows :], "blk", up)
    after = lax.ppermute(gathered[:, :after_rows], "blk", down)
    return jnp.concatenate([before, gathered, after], axis=1)


def conv_taps(padded, weight):
    row_count = padded.shape[1] - 2
    col_count = padded.shape[2]
    framed = jnp.pad(padded, ((0, 0), (0, 0), (1, 1)))
    running = jnp.zeros((weight.shape[2], row_count, col_count), jnp.float32)
    for row_tap in range(3):
        for col_tap in range(3):
            running = running + jnp.einsum(
                "oi,irw->orw",
                weight[row_tap, col_tap],
                framed[:, row_tap : row_tap + row_count, col_tap : col_tap + col_count],
                preferred_element_type=jnp.float32,
            )
    return running


def weight_taps(grad_out, padded):
    row_count = grad_out.shape[1]
    col_count = grad_out.shape[2]
    framed = jnp.pad(padded, ((0, 0), (0, 0), (1, 1)))
    stacked = []
    for row_tap in range(3):
        line = []
        for col_tap in range(3):
            line.append(
                jnp.einsum(
                    "orw,irw->oi",
                    grad_out,
                    framed[:, row_tap : row_tap + row_count, col_tap : col_tap + col_count],
                    preferred_element_type=jnp.float32,
                )
            )
        stacked.append(jnp.stack(line))
    return jnp.stack(stacked)


def spread_taps(grad_out, weight):
    row_count = grad_out.shape[1]
    col_count = grad_out.shape[2]
    framed = jnp.pad(grad_out, ((0, 0), (2, 2), (2, 2)))
    running = jnp.zeros((weight.shape[3], row_count + 2, col_count), jnp.float32)
    for row_tap in range(3):
        for col_tap in range(3):
            row_start = 2 - row_tap
            col_start = 3 - col_tap
            running = running + jnp.einsum(
                "oi,orw->irw",
                weight[row_tap, col_tap],
                framed[:, row_start : row_start + row_count + 2, col_start : col_start + col_count],
                preferred_element_type=jnp.float32,
            )
    return running


def spread_stride(grad_out, weight):
    out_rows = grad_out.shape[1]
    out_cols = grad_out.shape[2]
    channels = weight.shape[3]
    framed = jnp.pad(grad_out, ((0, 0), (1, 1), (1, 1)))
    parity_rows = []
    for row_par in range(2):
        parity_cols = []
        for col_par in range(2):
            running = jnp.zeros((channels, out_rows + 1, out_cols + 1), jnp.float32)
            for row_tap in range(row_par, 3, 2):
                for col_tap in range(col_par, 3, 2):
                    row_start = 1 - row_tap // 2
                    col_start = 1 - col_tap // 2
                    running = running + jnp.einsum(
                        "oi,orw->irw",
                        weight[row_tap, col_tap],
                        framed[
                            :,
                            row_start : row_start + out_rows + 1,
                            col_start : col_start + out_cols + 1,
                        ],
                        preferred_element_type=jnp.float32,
                    )
            parity_cols.append(running)
        parity_rows.append(jnp.stack(parity_cols, axis=3))
    woven = jnp.stack(parity_rows, axis=2)
    woven = woven.reshape(channels, 2 * out_rows + 2, 2 * out_cols + 2)
    return woven[:, : 2 * out_rows + 1, 1 : 2 * out_cols + 1]


def fold_rims(grad_rows, both_sides):
    interior = grad_rows[:, 1:-1] if both_sides else grad_rows[:, 1:]
    from_next = passed_along(grad_rows[:, :1].astype(jnp.bfloat16), "blk", -1).astype(jnp.float32)
    if both_sides:
        from_prev = passed_along(grad_rows[:, -1:].astype(jnp.bfloat16), "blk", 1).astype(
            jnp.float32
        )
        return jnp.concatenate(
            [interior[:, :1] + from_prev, interior[:, 1:-1], interior[:, -1:] + from_next], axis=1
        )
    return jnp.concatenate([interior[:, :-1], interior[:, -1:] + from_next], axis=1)


def own_inputs(weight):
    whole = lax.all_gather(weight, "chan", axis=2, tiled=True)
    width = whole.shape[3] // lax.axis_size("chan")
    return lax.dynamic_slice_in_dim(whole, lax.axis_index("chan") * width, width, axis=3)


def input_grad(delta, weight):
    every = lax.all_gather(delta, "chan", axis=0, tiled=True)
    return fold_rims(spread_taps(every, weight), True)


def third_input_grad(upstream, weight):
    every = lax.all_gather(upstream, "chan", axis=0, tiled=True)
    return fold_rims(spread_stride(every, weight), False)


def parity_picker(cols, out_cols):
    source = lax.broadcasted_iota(jnp.int32, (cols, 3 * out_cols), 0)
    target = lax.broadcasted_iota(jnp.int32, (cols, 3 * out_cols), 1)
    wanted = 2 * (target % out_cols) + target // out_cols - 1
    return (source == wanted).astype(jnp.bfloat16)


def summed_over_cycle(parts, axis):
    devices = lax.axis_size(axis)
    flat = jnp.concatenate([p.reshape(-1) for p in parts])
    pieces = lax.all_to_all(flat.reshape(devices, -1), axis, 0, 0, tiled=True)
    total = jnp.sum(pieces, axis=0)
    spread = jnp.broadcast_to(total[None], (devices,) + total.shape)
    whole = lax.all_to_all(spread, axis, 0, 0, tiled=True).reshape(-1)
    out, start = [], 0
    for p in parts:
        out.append(whole[start : start + p.size].reshape(p.shape))
        start += p.size
    return out


def gelu_back(pre_act, grad_in):
    return jax.vjp(jax.nn.gelu, pre_act)[1](grad_in)[0]


def shards(inputs, w_first, w_second, w_third, cotangent, mirror):
    mirrored = mirror[0]
    oriented = orient(inputs, mirrored)
    upstream = orient(cotangent, mirrored)
    first_wide = widen_by(oriented, 3, 2)
    first_pre_wide = conv_taps(first_wide, w_first)
    first_act_wide = jax.nn.gelu(first_pre_wide).astype(jnp.bfloat16)
    first_pad = first_wide[:, 2:-1]
    first_pre = first_pre_wide[:, 2:-1]
    second_wide = lax.all_gather(first_act_wide, "chan", axis=0, tiled=True)
    second_pre_wide = conv_taps(second_wide, w_second)
    second_act_wide = jax.nn.gelu(second_pre_wide).astype(jnp.bfloat16)
    second_pad = second_wide[:, 1:]
    second_pre = second_pre_wide[:, 1:]
    stride_rows = lax.all_gather(second_act_wide, "chan", axis=0, tiled=True)
    out_rows = upstream.shape[1]
    out_cols = upstream.shape[2]
    by_parity = jnp.einsum(
        "irt,tk->irk",
        stride_rows,
        parity_picker(2 * out_cols, out_cols),
        preferred_element_type=jnp.float32,
    ).astype(jnp.bfloat16)
    spaced = jnp.stack([upstream, jnp.zeros_like(upstream)], axis=2).reshape(
        upstream.shape[0], 2 * out_rows, out_cols
    )
    row_placed = jnp.stack(
        [jnp.pad(spaced, ((0, 0), (row_tap, 1), (0, 0)))[:, : 2 * out_rows + 1] for row_tap in range(3)]
    )
    third_grad = jnp.stack(
        [
            jnp.einsum(
                "aosc,isc->aoi",
                row_placed,
                by_parity[:, :, col_tap * out_cols : (col_tap + 1) * out_cols],
                preferred_element_type=jnp.float32,
            )
            for col_tap in range(3)
        ],
        axis=1,
    )
    second_back = third_input_grad(upstream, own_inputs(w_third))
    second_delta = gelu_back(second_pre, second_back).astype(jnp.bfloat16)
    second_grad = weight_taps(second_delta, second_pad)
    first_back = input_grad(second_delta, own_inputs(w_second))
    first_delta = gelu_back(first_pre, first_back).astype(jnp.bfloat16)
    first_grad = weight_taps(first_delta, first_pad)
    input_back = input_grad(first_delta, own_inputs(w_first)).astype(jnp.bfloat16)
    reduced = summed_over_cycle((first_grad, second_grad, third_grad), "blk")
    cell_count = inputs.shape[1] * inputs.shape[2] * lax.axis_size("blk")
    return (
        orient(input_back, mirrored),
        reduced[0] / math.sqrt(cell_count),
        reduced[1] / math.sqrt(cell_count),
        reduced[2] / math.sqrt(cell_count // 4),
    )


def solution(mesh):
    placed = (
        P("chan", "blk", None),
        P(None, None, "chan", None),
        P(None, None, "chan", None),
        P(None, None, "chan", None),
        P("chan", "blk", None),
        P("blk"),
    )
    return jax.shard_map(
        shards,
        mesh=mesh,
        in_specs=placed,
        out_specs=(
            P("chan", "blk", None),
            P(None, None, "chan", None),
            P(None, None, "chan", None),
            P(None, None, "chan", None),
        ),
        check_vma=False,
    )
```

```python
import math

import jax
import jax.numpy as jnp
from jax import lax
from jax.sharding import PartitionSpec as P


def extended(shard, sides, width):
    for axis, dim in sides:
        devices, length = (lax.axis_size(axis), shard.shape[dim])
        up = [(i, (i + 1) % devices) for i in range(devices)]
        down = [(j, i) for i, j in up]
        last = lax.slice_in_dim(shard, length - width, length, axis=dim)
        leading = lax.slice_in_dim(shard, 0, width, axis=dim)
        before = lax.ppermute(last, axis, up)
        after = lax.ppermute(leading, axis, down)
        shard = jnp.concatenate([before, shard, after], axis=dim)
    return shard


def passed_along(shard, axis, by):
    devices = lax.axis_size(axis)
    return lax.ppermute(shard, axis, [(i, (i + by) % devices) for i in range(devices)])


def orient(block, mirrored):
    return jnp.where(mirrored == 1, block[..., ::-1], block)


def widen(active):
    gathered = lax.all_gather(active, "chan", axis=0, tiled=True)
    return extended(gathered, (("blk", 1),), 1)


def widen_by(active, before_rows, after_rows):
    gathered = lax.all_gather(active, "chan", axis=0, tiled=True)
    devices, length = lax.axis_size("blk"), gathered.shape[1]
    up = [(i, (i + 1) % devices) for i in range(devices)]
    down = [(j, i) for i, j in up]
    before = lax.ppermute(gathered[:, length - before_rows :], "blk", up)
    after = lax.ppermute(gathered[:, :after_rows], "blk", down)
    return jnp.concatenate([before, gathered, after], axis=1)


def conv_taps(padded, weight):
    row_count = padded.shape[1] - 2
    col_count = padded.shape[2]
    framed = jnp.pad(padded, ((0, 0), (0, 0), (1, 1)))
    running = jnp.zeros((weight.shape[2], row_count, col_count), jnp.float32)
    for row_tap in range(3):
        for col_tap in range(3):
            running = running + jnp.einsum(
                "oi,irw->orw",
                weight[row_tap, col_tap],
                framed[:, row_tap : row_tap + row_count, col_tap : col_tap + col_count],
                preferred_element_type=jnp.float32,
            )
    return running


def weight_taps(grad_out, padded):
    row_count = grad_out.shape[1]
    col_count = grad_out.shape[2]
    framed = jnp.pad(padded, ((0, 0), (0, 0), (1, 1)))
    stacked = []
    for row_tap in range(3):
        line = []
        for col_tap in range(3):
            line.append(
                jnp.einsum(
                    "orw,irw->oi",
                    grad_out,
                    framed[:, row_tap : row_tap + row_count, col_tap : col_tap + col_count],
                    preferred_element_type=jnp.float32,
                )
            )
        stacked.append(jnp.stack(line))
    return jnp.stack(stacked)


def spread_taps(grad_out, weight):
    row_count = grad_out.shape[1]
    col_count = grad_out.shape[2]
    framed = jnp.pad(grad_out, ((0, 0), (2, 2), (2, 2)))
    running = jnp.zeros((weight.shape[3], row_count + 2, col_count), jnp.float32)
    for row_tap in range(3):
        for col_tap in range(3):
            row_start = 2 - row_tap
            col_start = 3 - col_tap
            running = running + jnp.einsum(
                "oi,orw->irw",
                weight[row_tap, col_tap],
                framed[:, row_start : row_start + row_count + 2, col_start : col_start + col_count],
                preferred_element_type=jnp.float32,
            )
    return running


def spread_stride(grad_out, weight):
    out_rows = grad_out.shape[1]
    out_cols = grad_out.shape[2]
    channels = weight.shape[3]
    framed = jnp.pad(grad_out, ((0, 0), (1, 1), (1, 1)))
    parity_rows = []
    for row_par in range(2):
        parity_cols = []
        for col_par in range(2):
            running = jnp.zeros((channels, out_rows + 1, out_cols + 1), jnp.float32)
            for row_tap in range(row_par, 3, 2):
                for col_tap in range(col_par, 3, 2):
                    row_start = 1 - row_tap // 2
                    col_start = 1 - col_tap // 2
                    running = running + jnp.einsum(
                        "oi,orw->irw",
                        weight[row_tap, col_tap],
                        framed[
                            :,
                            row_start : row_start + out_rows + 1,
                            col_start : col_start + out_cols + 1,
                        ],
                        preferred_element_type=jnp.float32,
                    )
            parity_cols.append(running)
        parity_rows.append(jnp.stack(parity_cols, axis=3))
    woven = jnp.stack(parity_rows, axis=2)
    woven = woven.reshape(channels, 2 * out_rows + 2, 2 * out_cols + 2)
    return woven[:, : 2 * out_rows + 1, 1 : 2 * out_cols + 1]


def fold_rims(grad_rows, both_sides):
    interior = grad_rows[:, 1:-1] if both_sides else grad_rows[:, 1:]
    from_next = passed_along(grad_rows[:, :1].astype(jnp.bfloat16), "blk", -1).astype(jnp.float32)
    if both_sides:
        from_prev = passed_along(grad_rows[:, -1:].astype(jnp.bfloat16), "blk", 1).astype(
            jnp.float32
        )
        return jnp.concatenate(
            [interior[:, :1] + from_prev, interior[:, 1:-1], interior[:, -1:] + from_next], axis=1
        )
    return jnp.concatenate([interior[:, :-1], interior[:, -1:] + from_next], axis=1)


def own_inputs(weight):
    whole = lax.all_gather(weight, "chan", axis=2, tiled=True)
    width = whole.shape[3] // lax.axis_size("chan")
    return lax.dynamic_slice_in_dim(whole, lax.axis_index("chan") * width, width, axis=3)


def input_grad(delta, weight):
    every = lax.all_gather(delta, "chan", axis=0, tiled=True)
    return fold_rims(spread_taps(every, weight), True)


def third_input_grad(upstream, weight):
    every = lax.all_gather(upstream, "chan", axis=0, tiled=True)
    return fold_rims(spread_stride(every, weight), False)


def parity_picker(cols, out_cols):
    source = lax.broadcasted_iota(jnp.int32, (cols, 3 * out_cols), 0)
    target = lax.broadcasted_iota(jnp.int32, (cols, 3 * out_cols), 1)
    wanted = 2 * (target % out_cols) + target // out_cols - 1
    return (source == wanted).astype(jnp.bfloat16)


def summed_over_cycle(parts, axis):
    devices = lax.axis_size(axis)
    flat = jnp.concatenate([p.reshape(-1) for p in parts])
    pieces = lax.all_to_all(flat.reshape(devices, -1), axis, 0, 0, tiled=True)
    total = jnp.sum(pieces, axis=0)
    spread = jnp.broadcast_to(total[None], (devices,) + total.shape)
    whole = lax.all_to_all(spread, axis, 0, 0, tiled=True).reshape(-1)
    out, start = [], 0
    for p in parts:
        out.append(whole[start : start + p.size].reshape(p.shape))
        start += p.size
    return out


def gelu_back(pre_act, grad_in):
    return jax.vjp(jax.nn.gelu, pre_act)[1](grad_in)[0]


def shards(inputs, w_first, w_second, w_third, cotangent, mirror):
    mirrored = mirror[0]
    oriented = orient(inputs, mirrored)
    upstream = orient(cotangent, mirrored)
    first_wide = widen_by(oriented, 4, 4)
    first_pre_wide = conv_taps(first_wide, w_first)
    first_act_wide = jax.nn.gelu(first_pre_wide).astype(jnp.bfloat16)
    first_pad = first_wide[:, 3:-3]
    first_pre = first_pre_wide[:, 2:-2]
    second_wide = lax.all_gather(first_act_wide, "chan", axis=0, tiled=True)
    second_pre_wide = conv_taps(second_wide, w_second)
    second_act_wide = jax.nn.gelu(second_pre_wide).astype(jnp.bfloat16)
    second_pad = second_wide[:, 2:-2]
    stride_rows = lax.all_gather(second_act_wide, "chan", axis=0, tiled=True)[:, 1:-2]
    out_rows = upstream.shape[1]
    out_cols = upstream.shape[2]
    by_parity = jnp.einsum(
        "irt,tk->irk",
        stride_rows,
        parity_picker(2 * out_cols, out_cols),
        preferred_element_type=jnp.float32,
    ).astype(jnp.bfloat16)
    spaced = jnp.stack([upstream, jnp.zeros_like(upstream)], axis=2).reshape(
        upstream.shape[0], 2 * out_rows, out_cols
    )
    row_placed = jnp.stack(
        [jnp.pad(spaced, ((0, 0), (row_tap, 1), (0, 0)))[:, : 2 * out_rows + 1] for row_tap in range(3)]
    )
    third_grad = jnp.stack(
        [
            jnp.einsum(
                "aosc,isc->aoi",
                row_placed,
                by_parity[:, :, col_tap * out_cols : (col_tap + 1) * out_cols],
                preferred_element_type=jnp.float32,
            )
            for col_tap in range(3)
        ],
        axis=1,
    )
    upstream_wide = widen_by(upstream, 1, 2)
    second_back = spread_stride(upstream_wide, own_inputs(w_third))[:, 1:-2]
    second_delta_wide = gelu_back(second_pre_wide, second_back).astype(jnp.bfloat16)
    second_delta = second_delta_wide[:, 2:-2]
    second_grad = weight_taps(second_delta, second_pad)
    delta_all = lax.all_gather(second_delta_wide, "chan", axis=0, tiled=True)
    first_back = spread_taps(delta_all, own_inputs(w_second))[:, 2:-2]
    first_delta_wide = gelu_back(first_pre, first_back).astype(jnp.bfloat16)
    first_delta = first_delta_wide[:, 1:-1]
    first_grad = weight_taps(first_delta, first_pad)
    delta_all = lax.all_gather(first_delta_wide, "chan", axis=0, tiled=True)
    input_back = spread_taps(delta_all, own_inputs(w_first))[:, 2:-2].astype(jnp.bfloat16)
    reduced = summed_over_cycle((first_grad, second_grad, third_grad), "blk")
    cell_count = inputs.shape[1] * inputs.shape[2] * lax.axis_size("blk")
    return (
        orient(input_back, mirrored),
        reduced[0] / math.sqrt(cell_count),
        reduced[1] / math.sqrt(cell_count),
        reduced[2] / math.sqrt(cell_count // 4),
    )


def solution(mesh):
    placed = (
        P("chan", "blk", None),
        P(None, None, "chan", None),
        P(None, None, "chan", None),
        P(None, None, "chan", None),
        P("chan", "blk", None),
        P("blk"),
    )
    return jax.shard_map(
        shards,
        mesh=mesh,
        in_specs=placed,
        out_specs=(
            P("chan", "blk", None),
            P(None, None, "chan", None),
            P(None, None, "chan", None),
            P(None, None, "chan", None),
        ),
        check_vma=False,
    )
```

```python
import math

import jax
import jax.numpy as jnp
from jax import lax
from jax.sharding import PartitionSpec as P


def extended(shard, sides, width):
    for axis, dim in sides:
        devices, length = (lax.axis_size(axis), shard.shape[dim])
        up = [(i, (i + 1) % devices) for i in range(devices)]
        down = [(j, i) for i, j in up]
        last = lax.slice_in_dim(shard, length - width, length, axis=dim)
        leading = lax.slice_in_dim(shard, 0, width, axis=dim)
        before = lax.ppermute(last, axis, up)
        after = lax.ppermute(leading, axis, down)
        shard = jnp.concatenate([before, shard, after], axis=dim)
    return shard


def passed_along(shard, axis, by):
    devices = lax.axis_size(axis)
    return lax.ppermute(shard, axis, [(i, (i + by) % devices) for i in range(devices)])


def orient(block, mirrored):
    return jnp.where(mirrored == 1, block[..., ::-1], block)


def widen(active):
    gathered = lax.all_gather(active, "chan", axis=0, tiled=True)
    return extended(gathered, (("blk", 1),), 1)


def gathered_rows(active, rows=4):
    pieces = [
        lax.all_gather(active[:, start : start + rows], "chan", axis=0, tiled=True)
        for start in range(0, active.shape[1], rows)
    ]
    return jnp.concatenate(pieces, axis=1)


def widen_by(active, before_rows, after_rows):
    gathered = gathered_rows(active)
    devices, length = lax.axis_size("blk"), gathered.shape[1]
    up = [(i, (i + 1) % devices) for i in range(devices)]
    down = [(j, i) for i, j in up]
    before = lax.ppermute(gathered[:, length - before_rows :], "blk", up)
    after = lax.ppermute(gathered[:, :after_rows], "blk", down)
    return jnp.concatenate([before, gathered, after], axis=1)


def conv_taps(padded, weight):
    row_count = padded.shape[1] - 2
    col_count = padded.shape[2]
    framed = jnp.pad(padded, ((0, 0), (0, 0), (1, 1)))
    running = jnp.zeros((weight.shape[2], row_count, col_count), jnp.float32)
    for row_tap in range(3):
        for col_tap in range(3):
            running = running + jnp.einsum(
                "oi,irw->orw",
                weight[row_tap, col_tap],
                framed[:, row_tap : row_tap + row_count, col_tap : col_tap + col_count],
                preferred_element_type=jnp.float32,
            )
    return running


def weight_taps(grad_out, padded):
    row_count = grad_out.shape[1]
    col_count = grad_out.shape[2]
    framed = jnp.pad(padded, ((0, 0), (0, 0), (1, 1)))
    stacked = []
    for row_tap in range(3):
        line = []
        for col_tap in range(3):
            line.append(
                jnp.einsum(
                    "orw,irw->oi",
                    grad_out,
                    framed[:, row_tap : row_tap + row_count, col_tap : col_tap + col_count],
                    preferred_element_type=jnp.float32,
                )
            )
        stacked.append(jnp.stack(line))
    return jnp.stack(stacked)


def spread_taps(grad_out, weight):
    row_count = grad_out.shape[1]
    col_count = grad_out.shape[2]
    framed = jnp.pad(grad_out, ((0, 0), (2, 2), (2, 2)))
    running = jnp.zeros((weight.shape[3], row_count + 2, col_count), jnp.float32)
    for row_tap in range(3):
        for col_tap in range(3):
            row_start = 2 - row_tap
            col_start = 3 - col_tap
            running = running + jnp.einsum(
                "oi,orw->irw",
                weight[row_tap, col_tap],
                framed[:, row_start : row_start + row_count + 2, col_start : col_start + col_count],
                preferred_element_type=jnp.float32,
            )
    return running


def spread_stride(grad_out, weight):
    out_rows = grad_out.shape[1]
    out_cols = grad_out.shape[2]
    channels = weight.shape[3]
    framed = jnp.pad(grad_out, ((0, 0), (1, 1), (1, 1)))
    parity_rows = []
    for row_par in range(2):
        parity_cols = []
        for col_par in range(2):
            running = jnp.zeros((channels, out_rows + 1, out_cols + 1), jnp.float32)
            for row_tap in range(row_par, 3, 2):
                for col_tap in range(col_par, 3, 2):
                    row_start = 1 - row_tap // 2
                    col_start = 1 - col_tap // 2
                    running = running + jnp.einsum(
                        "oi,orw->irw",
                        weight[row_tap, col_tap],
                        framed[
                            :,
                            row_start : row_start + out_rows + 1,
                            col_start : col_start + out_cols + 1,
                        ],
                        preferred_element_type=jnp.float32,
                    )
            parity_cols.append(running)
        parity_rows.append(jnp.stack(parity_cols, axis=3))
    woven = jnp.stack(parity_rows, axis=2)
    woven = woven.reshape(channels, 2 * out_rows + 2, 2 * out_cols + 2)
    return woven[:, : 2 * out_rows + 1, 1 : 2 * out_cols + 1]


def fold_rims(grad_rows, both_sides):
    interior = grad_rows[:, 1:-1] if both_sides else grad_rows[:, 1:]
    from_next = passed_along(grad_rows[:, :1].astype(jnp.bfloat16), "blk", -1).astype(jnp.float32)
    if both_sides:
        from_prev = passed_along(grad_rows[:, -1:].astype(jnp.bfloat16), "blk", 1).astype(
            jnp.float32
        )
        return jnp.concatenate(
            [interior[:, :1] + from_prev, interior[:, 1:-1], interior[:, -1:] + from_next], axis=1
        )
    return jnp.concatenate([interior[:, :-1], interior[:, -1:] + from_next], axis=1)


def own_inputs(weight):
    whole = lax.all_gather(weight, "chan", axis=2, tiled=True)
    width = whole.shape[3] // lax.axis_size("chan")
    return lax.dynamic_slice_in_dim(whole, lax.axis_index("chan") * width, width, axis=3)


def input_grad(delta, weight):
    every = lax.all_gather(delta, "chan", axis=0, tiled=True)
    return fold_rims(spread_taps(every, weight), True)


def third_input_grad(upstream, weight):
    every = lax.all_gather(upstream, "chan", axis=0, tiled=True)
    return fold_rims(spread_stride(every, weight), False)


def parity_picker(cols, out_cols):
    source = lax.broadcasted_iota(jnp.int32, (cols, 3 * out_cols), 0)
    target = lax.broadcasted_iota(jnp.int32, (cols, 3 * out_cols), 1)
    wanted = 2 * (target % out_cols) + target // out_cols - 1
    return (source == wanted).astype(jnp.bfloat16)


def summed_over_cycle(parts, axis):
    devices = lax.axis_size(axis)
    flat = jnp.concatenate([p.reshape(-1) for p in parts])
    pieces = lax.all_to_all(flat.reshape(devices, -1), axis, 0, 0, tiled=True)
    total = jnp.sum(pieces, axis=0)
    spread = jnp.broadcast_to(total[None], (devices,) + total.shape)
    whole = lax.all_to_all(spread, axis, 0, 0, tiled=True).reshape(-1)
    out, start = [], 0
    for p in parts:
        out.append(whole[start : start + p.size].reshape(p.shape))
        start += p.size
    return out


def gelu_back(pre_act, grad_in):
    return jax.vjp(jax.nn.gelu, pre_act)[1](grad_in)[0]


def shards(inputs, w_first, w_second, w_third, cotangent, mirror):
    mirrored = mirror[0]
    oriented = orient(inputs, mirrored)
    upstream = orient(cotangent, mirrored)
    first_wide = widen_by(oriented, 4, 4)
    first_pre_wide = conv_taps(first_wide, w_first)
    first_act_wide = jax.nn.gelu(first_pre_wide).astype(jnp.bfloat16)
    first_pad = first_wide[:, 3:-3]
    first_pre = first_pre_wide[:, 2:-2]
    second_wide = gathered_rows(first_act_wide)
    second_pre_wide = conv_taps(second_wide, w_second)
    second_act_wide = jax.nn.gelu(second_pre_wide).astype(jnp.bfloat16)
    second_pad = second_wide[:, 2:-2]
    stride_rows = gathered_rows(second_act_wide)[:, 1:-2]
    out_rows = upstream.shape[1]
    out_cols = upstream.shape[2]
    by_parity = jnp.einsum(
        "irt,tk->irk",
        stride_rows,
        parity_picker(2 * out_cols, out_cols),
        preferred_element_type=jnp.float32,
    ).astype(jnp.bfloat16)
    spaced = jnp.stack([upstream, jnp.zeros_like(upstream)], axis=2).reshape(
        upstream.shape[0], 2 * out_rows, out_cols
    )
    row_placed = jnp.stack(
        [jnp.pad(spaced, ((0, 0), (row_tap, 1), (0, 0)))[:, : 2 * out_rows + 1] for row_tap in range(3)]
    )
    third_grad = jnp.stack(
        [
            jnp.einsum(
                "aosc,isc->aoi",
                row_placed,
                by_parity[:, :, col_tap * out_cols : (col_tap + 1) * out_cols],
                preferred_element_type=jnp.float32,
            )
            for col_tap in range(3)
        ],
        axis=1,
    )
    upstream_wide = widen_by(upstream, 1, 2)
    second_back = spread_stride(upstream_wide, own_inputs(w_third))[:, 1:-2]
    second_delta_wide = gelu_back(second_pre_wide, second_back).astype(jnp.bfloat16)
    second_delta = second_delta_wide[:, 2:-2]
    second_grad = weight_taps(second_delta, second_pad)
    delta_all = gathered_rows(second_delta_wide)
    first_back = spread_taps(delta_all, own_inputs(w_second))[:, 2:-2]
    first_delta_wide = gelu_back(first_pre, first_back).astype(jnp.bfloat16)
    first_delta = first_delta_wide[:, 1:-1]
    first_grad = weight_taps(first_delta, first_pad)
    delta_all = gathered_rows(first_delta_wide)
    input_back = spread_taps(delta_all, own_inputs(w_first))[:, 2:-2].astype(jnp.bfloat16)
    reduced = summed_over_cycle((first_grad, second_grad, third_grad), "blk")
    cell_count = inputs.shape[1] * inputs.shape[2] * lax.axis_size("blk")
    return (
        orient(input_back, mirrored),
        reduced[0] / math.sqrt(cell_count),
        reduced[1] / math.sqrt(cell_count),
        reduced[2] / math.sqrt(cell_count // 4),
    )


def solution(mesh):
    placed = (
        P("chan", "blk", None),
        P(None, None, "chan", None),
        P(None, None, "chan", None),
        P(None, None, "chan", None),
        P("chan", "blk", None),
        P("blk"),
    )
    return jax.shard_map(
        shards,
        mesh=mesh,
        in_specs=placed,
        out_specs=(
            P("chan", "blk", None),
            P(None, None, "chan", None),
            P(None, None, "chan", None),
            P(None, None, "chan", None),
        ),
        check_vma=False,
    )
```

```python
import math

import jax
import jax.numpy as jnp
from jax import lax
from jax.sharding import PartitionSpec as P


def extended(shard, sides, width):
    for axis, dim in sides:
        devices, length = (lax.axis_size(axis), shard.shape[dim])
        up = [(i, (i + 1) % devices) for i in range(devices)]
        down = [(j, i) for i, j in up]
        last = lax.slice_in_dim(shard, length - width, length, axis=dim)
        leading = lax.slice_in_dim(shard, 0, width, axis=dim)
        before = lax.ppermute(last, axis, up)
        after = lax.ppermute(leading, axis, down)
        shard = jnp.concatenate([before, shard, after], axis=dim)
    return shard


def passed_along(shard, axis, by):
    devices = lax.axis_size(axis)
    return lax.ppermute(shard, axis, [(i, (i + by) % devices) for i in range(devices)])


def orient(block, mirrored):
    return jnp.where(mirrored == 1, block[..., ::-1], block)


def widen(active):
    gathered = lax.all_gather(active, "chan", axis=0, tiled=True)
    return extended(gathered, (("blk", 1),), 1)


def widen_by(active, before_rows, after_rows):
    gathered = lax.all_gather(active, "chan", axis=0, tiled=True)
    devices, length = lax.axis_size("blk"), gathered.shape[1]
    up = [(i, (i + 1) % devices) for i in range(devices)]
    down = [(j, i) for i, j in up]
    before = lax.ppermute(gathered[:, length - before_rows :], "blk", up)
    after = lax.ppermute(gathered[:, :after_rows], "blk", down)
    return jnp.concatenate([before, gathered, after], axis=1)


def conv_taps(padded, weight):
    row_count = padded.shape[1] - 2
    col_count = padded.shape[2]
    framed = jnp.pad(padded, ((0, 0), (0, 0), (1, 1)))
    running = jnp.zeros((weight.shape[2], row_count, col_count), jnp.float32)
    for row_tap in range(3):
        for col_tap in range(3):
            running = running + jnp.einsum(
                "oi,irw->orw",
                weight[row_tap, col_tap],
                framed[:, row_tap : row_tap + row_count, col_tap : col_tap + col_count],
                preferred_element_type=jnp.float32,
            )
    return running


def weight_taps(grad_out, padded):
    row_count = grad_out.shape[1]
    col_count = grad_out.shape[2]
    framed = jnp.pad(padded, ((0, 0), (0, 0), (1, 1)))
    stacked = []
    for row_tap in range(3):
        line = []
        for col_tap in range(3):
            line.append(
                jnp.einsum(
                    "orw,irw->oi",
                    grad_out,
                    framed[:, row_tap : row_tap + row_count, col_tap : col_tap + col_count],
                    preferred_element_type=jnp.float32,
                )
            )
        stacked.append(jnp.stack(line))
    return jnp.stack(stacked)


def spread_taps(grad_out, weight):
    row_count = grad_out.shape[1]
    col_count = grad_out.shape[2]
    framed = jnp.pad(grad_out, ((0, 0), (2, 2), (2, 2)))
    running = jnp.zeros((weight.shape[3], row_count + 2, col_count), jnp.float32)
    for row_tap in range(3):
        for col_tap in range(3):
            row_start = 2 - row_tap
            col_start = 3 - col_tap
            running = running + jnp.einsum(
                "oi,orw->irw",
                weight[row_tap, col_tap],
                framed[:, row_start : row_start + row_count + 2, col_start : col_start + col_count],
                preferred_element_type=jnp.float32,
            )
    return running


def spread_stride(grad_out, weight):
    out_rows = grad_out.shape[1]
    out_cols = grad_out.shape[2]
    channels = weight.shape[3]
    framed = jnp.pad(grad_out, ((0, 0), (1, 1), (1, 1)))
    parity_rows = []
    for row_par in range(2):
        parity_cols = []
        for col_par in range(2):
            running = jnp.zeros((channels, out_rows + 1, out_cols + 1), jnp.float32)
            for row_tap in range(row_par, 3, 2):
                for col_tap in range(col_par, 3, 2):
                    row_start = 1 - row_tap // 2
                    col_start = 1 - col_tap // 2
                    running = running + jnp.einsum(
                        "oi,orw->irw",
                        weight[row_tap, col_tap],
                        framed[
                            :,
                            row_start : row_start + out_rows + 1,
                            col_start : col_start + out_cols + 1,
                        ],
                        preferred_element_type=jnp.float32,
                    )
            parity_cols.append(running)
        parity_rows.append(jnp.stack(parity_cols, axis=3))
    woven = jnp.stack(parity_rows, axis=2)
    woven = woven.reshape(channels, 2 * out_rows + 2, 2 * out_cols + 2)
    return woven[:, : 2 * out_rows + 1, 1 : 2 * out_cols + 1]


def fold_rims(grad_rows, both_sides):
    interior = grad_rows[:, 1:-1] if both_sides else grad_rows[:, 1:]
    from_next = passed_along(grad_rows[:, :1].astype(jnp.bfloat16), "blk", -1).astype(jnp.float32)
    if both_sides:
        from_prev = passed_along(grad_rows[:, -1:].astype(jnp.bfloat16), "blk", 1).astype(
            jnp.float32
        )
        return jnp.concatenate(
            [interior[:, :1] + from_prev, interior[:, 1:-1], interior[:, -1:] + from_next], axis=1
        )
    return jnp.concatenate([interior[:, :-1], interior[:, -1:] + from_next], axis=1)


def own_inputs(weights):
    sizes = [w.shape[2] for w in weights]
    devices = lax.axis_size("chan")
    whole = lax.all_gather(jnp.concatenate(weights, axis=2), "chan", axis=0, tiled=False)
    width = weights[0].shape[3] // devices
    mine = lax.dynamic_slice_in_dim(whole, lax.axis_index("chan") * width, width, axis=4)
    out, start = [], 0
    for size in sizes:
        parts = [mine[d, :, :, start : start + size] for d in range(devices)]
        out.append(jnp.concatenate(parts, axis=2))
        start += size
    return out


def input_grad(delta, weight):
    every = lax.all_gather(delta, "chan", axis=0, tiled=True)
    return fold_rims(spread_taps(every, weight), True)


def third_input_grad(upstream, weight):
    every = lax.all_gather(upstream, "chan", axis=0, tiled=True)
    return fold_rims(spread_stride(every, weight), False)


def parity_picker(cols, out_cols):
    source = lax.broadcasted_iota(jnp.int32, (cols, 3 * out_cols), 0)
    target = lax.broadcasted_iota(jnp.int32, (cols, 3 * out_cols), 1)
    wanted = 2 * (target % out_cols) + target // out_cols - 1
    return (source == wanted).astype(jnp.bfloat16)


def summed_over_cycle(parts, axis):
    devices = lax.axis_size(axis)
    flat = jnp.concatenate([p.reshape(-1) for p in parts])
    pieces = lax.all_to_all(flat.reshape(devices, -1), axis, 0, 0, tiled=True)
    total = jnp.sum(pieces, axis=0)
    spread = jnp.broadcast_to(total[None], (devices,) + total.shape)
    whole = lax.all_to_all(spread, axis, 0, 0, tiled=True).reshape(-1)
    out, start = [], 0
    for p in parts:
        out.append(whole[start : start + p.size].reshape(p.shape))
        start += p.size
    return out


def gelu_back(pre_act, grad_in):
    return jax.vjp(jax.nn.gelu, pre_act)[1](grad_in)[0]


def shards(inputs, w_first, w_second, w_third, cotangent, mirror):
    mirrored = mirror[0]
    oriented = orient(inputs, mirrored)
    upstream = orient(cotangent, mirrored)
    first_wide = widen_by(oriented, 3, 2)
    first_pre_wide = conv_taps(first_wide, w_first)
    first_act_wide = jax.nn.gelu(first_pre_wide).astype(jnp.bfloat16)
    first_pad = first_wide[:, 2:-1]
    first_pre = first_pre_wide[:, 2:-1]
    second_wide = lax.all_gather(first_act_wide, "chan", axis=0, tiled=True)
    second_pre_wide = conv_taps(second_wide, w_second)
    second_act_wide = jax.nn.gelu(second_pre_wide).astype(jnp.bfloat16)
    second_pad = second_wide[:, 1:]
    second_pre = second_pre_wide[:, 1:]
    stride_rows = lax.all_gather(second_act_wide, "chan", axis=0, tiled=True)
    out_rows = upstream.shape[1]
    out_cols = upstream.shape[2]
    by_parity = jnp.einsum(
        "irt,tk->irk",
        stride_rows,
        parity_picker(2 * out_cols, out_cols),
        preferred_element_type=jnp.float32,
    ).astype(jnp.bfloat16)
    spaced = jnp.stack([upstream, jnp.zeros_like(upstream)], axis=2).reshape(
        upstream.shape[0], 2 * out_rows, out_cols
    )
    row_placed = jnp.stack(
        [jnp.pad(spaced, ((0, 0), (row_tap, 1), (0, 0)))[:, : 2 * out_rows + 1] for row_tap in range(3)]
    )
    third_grad = jnp.stack(
        [
            jnp.einsum(
                "aosc,isc->aoi",
                row_placed,
                by_parity[:, :, col_tap * out_cols : (col_tap + 1) * out_cols],
                preferred_element_type=jnp.float32,
            )
            for col_tap in range(3)
        ],
        axis=1,
    )
    first_mine, second_mine, third_mine = own_inputs((w_first, w_second, w_third))
    second_back = third_input_grad(upstream, third_mine)
    second_delta = gelu_back(second_pre, second_back).astype(jnp.bfloat16)
    second_grad = weight_taps(second_delta, second_pad)
    first_back = input_grad(second_delta, second_mine)
    first_delta = gelu_back(first_pre, first_back).astype(jnp.bfloat16)
    first_grad = weight_taps(first_delta, first_pad)
    input_back = input_grad(first_delta, first_mine).astype(jnp.bfloat16)
    reduced = summed_over_cycle((first_grad, second_grad, third_grad), "blk")
    cell_count = inputs.shape[1] * inputs.shape[2] * lax.axis_size("blk")
    return (
        orient(input_back, mirrored),
        reduced[0] / math.sqrt(cell_count),
        reduced[1] / math.sqrt(cell_count),
        reduced[2] / math.sqrt(cell_count // 4),
    )


def solution(mesh):
    placed = (
        P("chan", "blk", None),
        P(None, None, "chan", None),
        P(None, None, "chan", None),
        P(None, None, "chan", None),
        P("chan", "blk", None),
        P("blk"),
    )
    return jax.shard_map(
        shards,
        mesh=mesh,
        in_specs=placed,
        out_specs=(
            P("chan", "blk", None),
            P(None, None, "chan", None),
            P(None, None, "chan", None),
            P(None, None, "chan", None),
        ),
        check_vma=False,
    )
```

```python
import math

import jax
import jax.numpy as jnp
from jax import lax
from jax.sharding import PartitionSpec as P


def extended(shard, sides, width):
    for axis, dim in sides:
        devices, length = (lax.axis_size(axis), shard.shape[dim])
        up = [(i, (i + 1) % devices) for i in range(devices)]
        down = [(j, i) for i, j in up]
        last = lax.slice_in_dim(shard, length - width, length, axis=dim)
        leading = lax.slice_in_dim(shard, 0, width, axis=dim)
        before = lax.ppermute(last, axis, up)
        after = lax.ppermute(leading, axis, down)
        shard = jnp.concatenate([before, shard, after], axis=dim)
    return shard


def passed_along(shard, axis, by):
    devices = lax.axis_size(axis)
    return lax.ppermute(shard, axis, [(i, (i + by) % devices) for i in range(devices)])


def orient(block, mirrored):
    return jnp.where(mirrored == 1, block[..., ::-1], block)


def widen(active):
    gathered = lax.all_gather(active, "chan", axis=0, tiled=True)
    return extended(gathered, (("blk", 1),), 1)


def widen_by(active, before_rows, after_rows):
    gathered = lax.all_gather(active, "chan", axis=0, tiled=True)
    devices, length = lax.axis_size("blk"), gathered.shape[1]
    up = [(i, (i + 1) % devices) for i in range(devices)]
    down = [(j, i) for i, j in up]
    before = lax.ppermute(gathered[:, length - before_rows :], "blk", up)
    after = lax.ppermute(gathered[:, :after_rows], "blk", down)
    return jnp.concatenate([before, gathered, after], axis=1)


def conv_taps(padded, weight):
    row_count = padded.shape[1] - 2
    col_count = padded.shape[2]
    framed = jnp.pad(padded, ((0, 0), (0, 0), (1, 1)))
    running = jnp.zeros((weight.shape[2], row_count, col_count), jnp.float32)
    for row_tap in range(3):
        for col_tap in range(3):
            running = running + jnp.einsum(
                "oi,irw->orw",
                weight[row_tap, col_tap],
                framed[:, row_tap : row_tap + row_count, col_tap : col_tap + col_count],
                preferred_element_type=jnp.float32,
            )
    return running


def weight_taps(grad_out, padded):
    row_count = grad_out.shape[1]
    col_count = grad_out.shape[2]
    framed = jnp.pad(padded, ((0, 0), (0, 0), (1, 1)))
    stacked = []
    for row_tap in range(3):
        line = []
        for col_tap in range(3):
            line.append(
                jnp.einsum(
                    "orw,irw->oi",
                    grad_out,
                    framed[:, row_tap : row_tap + row_count, col_tap : col_tap + col_count],
                    preferred_element_type=jnp.float32,
                )
            )
        stacked.append(jnp.stack(line))
    return jnp.stack(stacked)


def spread_taps(grad_out, weight):
    row_count = grad_out.shape[1]
    col_count = grad_out.shape[2]
    framed = jnp.pad(grad_out, ((0, 0), (2, 2), (2, 2)))
    running = jnp.zeros((weight.shape[3], row_count + 2, col_count), jnp.float32)
    for row_tap in range(3):
        for col_tap in range(3):
            row_start = 2 - row_tap
            col_start = 3 - col_tap
            running = running + jnp.einsum(
                "oi,orw->irw",
                weight[row_tap, col_tap],
                framed[:, row_start : row_start + row_count + 2, col_start : col_start + col_count],
                preferred_element_type=jnp.float32,
            )
    return running


def spread_stride(grad_out, weight):
    out_rows = grad_out.shape[1]
    out_cols = grad_out.shape[2]
    channels = weight.shape[3]
    framed = jnp.pad(grad_out, ((0, 0), (1, 1), (1, 1)))
    parity_rows = []
    for row_par in range(2):
        parity_cols = []
        for col_par in range(2):
            running = jnp.zeros((channels, out_rows + 1, out_cols + 1), jnp.float32)
            for row_tap in range(row_par, 3, 2):
                for col_tap in range(col_par, 3, 2):
                    row_start = 1 - row_tap // 2
                    col_start = 1 - col_tap // 2
                    running = running + jnp.einsum(
                        "oi,orw->irw",
                        weight[row_tap, col_tap],
                        framed[
                            :,
                            row_start : row_start + out_rows + 1,
                            col_start : col_start + out_cols + 1,
                        ],
                        preferred_element_type=jnp.float32,
                    )
            parity_cols.append(running)
        parity_rows.append(jnp.stack(parity_cols, axis=3))
    woven = jnp.stack(parity_rows, axis=2)
    woven = woven.reshape(channels, 2 * out_rows + 2, 2 * out_cols + 2)
    return woven[:, : 2 * out_rows + 1, 1 : 2 * out_cols + 1]


def fold_rims(grad_rows, both_sides):
    interior = grad_rows[:, 1:-1] if both_sides else grad_rows[:, 1:]
    from_next = passed_along(grad_rows[:, :1].astype(jnp.bfloat16), "blk", -1).astype(jnp.float32)
    if both_sides:
        from_prev = passed_along(grad_rows[:, -1:].astype(jnp.bfloat16), "blk", 1).astype(
            jnp.float32
        )
        return jnp.concatenate(
            [interior[:, :1] + from_prev, interior[:, 1:-1], interior[:, -1:] + from_next], axis=1
        )
    return jnp.concatenate([interior[:, :-1], interior[:, -1:] + from_next], axis=1)


def own_inputs(weight):
    whole = lax.all_gather(weight, "chan", axis=2, tiled=True)
    width = whole.shape[3] // lax.axis_size("chan")
    return lax.dynamic_slice_in_dim(whole, lax.axis_index("chan") * width, width, axis=3)


def input_grad(delta, weight):
    every = lax.all_gather(delta, "chan", axis=0, tiled=True)
    return fold_rims(spread_taps(every, weight), True)


def third_input_grad(upstream, weight):
    every = lax.all_gather(upstream, "chan", axis=0, tiled=True)
    return fold_rims(spread_stride(every, weight), False)


def parity_picker(cols, out_cols):
    source = lax.broadcasted_iota(jnp.int32, (cols, 3 * out_cols), 0)
    target = lax.broadcasted_iota(jnp.int32, (cols, 3 * out_cols), 1)
    wanted = 2 * (target % out_cols) + target // out_cols - 1
    return (source == wanted).astype(jnp.bfloat16)


def summed_over_cycle(parts, axis, finished):
    devices = lax.axis_size(axis)
    flat = jnp.concatenate([p.reshape(-1) for p in parts])
    pieces = lax.all_to_all(flat.reshape(devices, -1), axis, 0, 0, tiled=True)
    total, finished = lax.optimization_barrier((jnp.sum(pieces, axis=0), finished))
    spread = jnp.broadcast_to(total[None], (devices,) + total.shape)
    whole = lax.all_to_all(spread, axis, 0, 0, tiled=True).reshape(-1)
    out, start = [], 0
    for p in parts:
        out.append(whole[start : start + p.size].reshape(p.shape))
        start += p.size
    return out, finished


def gelu_back(pre_act, grad_in):
    return jax.vjp(jax.nn.gelu, pre_act)[1](grad_in)[0]


def shards(inputs, w_first, w_second, w_third, cotangent, mirror):
    mirrored = mirror[0]
    oriented = orient(inputs, mirrored)
    upstream = orient(cotangent, mirrored)
    first_wide = widen_by(oriented, 3, 2)
    first_pre_wide = conv_taps(first_wide, w_first)
    first_act_wide = jax.nn.gelu(first_pre_wide).astype(jnp.bfloat16)
    first_pad = first_wide[:, 2:-1]
    first_pre = first_pre_wide[:, 2:-1]
    second_wide = lax.all_gather(first_act_wide, "chan", axis=0, tiled=True)
    second_pre_wide = conv_taps(second_wide, w_second)
    second_act_wide = jax.nn.gelu(second_pre_wide).astype(jnp.bfloat16)
    second_pad = second_wide[:, 1:]
    second_pre = second_pre_wide[:, 1:]
    stride_rows = lax.all_gather(second_act_wide, "chan", axis=0, tiled=True)
    out_rows = upstream.shape[1]
    out_cols = upstream.shape[2]
    by_parity = jnp.einsum(
        "irt,tk->irk",
        stride_rows,
        parity_picker(2 * out_cols, out_cols),
        preferred_element_type=jnp.float32,
    ).astype(jnp.bfloat16)
    spaced = jnp.stack([upstream, jnp.zeros_like(upstream)], axis=2).reshape(
        upstream.shape[0], 2 * out_rows, out_cols
    )
    row_placed = jnp.stack(
        [jnp.pad(spaced, ((0, 0), (row_tap, 1), (0, 0)))[:, : 2 * out_rows + 1] for row_tap in range(3)]
    )
    third_grad = jnp.stack(
        [
            jnp.einsum(
                "aosc,isc->aoi",
                row_placed,
                by_parity[:, :, col_tap * out_cols : (col_tap + 1) * out_cols],
                preferred_element_type=jnp.float32,
            )
            for col_tap in range(3)
        ],
        axis=1,
    )
    second_back = third_input_grad(upstream, own_inputs(w_third))
    second_delta = gelu_back(second_pre, second_back).astype(jnp.bfloat16)
    second_grad = weight_taps(second_delta, second_pad)
    first_back = input_grad(second_delta, own_inputs(w_second))
    first_delta = gelu_back(first_pre, first_back).astype(jnp.bfloat16)
    first_grad = weight_taps(first_delta, first_pad)
    input_back = input_grad(first_delta, own_inputs(w_first)).astype(jnp.bfloat16)
    reduced, input_back = summed_over_cycle((first_grad, second_grad, third_grad), "blk", input_back)
    cell_count = inputs.shape[1] * inputs.shape[2] * lax.axis_size("blk")
    return (
        orient(input_back, mirrored),
        reduced[0] / math.sqrt(cell_count),
        reduced[1] / math.sqrt(cell_count),
        reduced[2] / math.sqrt(cell_count // 4),
    )


def solution(mesh):
    placed = (
        P("chan", "blk", None),
        P(None, None, "chan", None),
        P(None, None, "chan", None),
        P(None, None, "chan", None),
        P("chan", "blk", None),
        P("blk"),
    )
    return jax.shard_map(
        shards,
        mesh=mesh,
        in_specs=placed,
        out_specs=(
            P("chan", "blk", None),
            P(None, None, "chan", None),
            P(None, None, "chan", None),
            P(None, None, "chan", None),
        ),
        check_vma=False,
    )
```

```python
import math

import jax
import jax.numpy as jnp
from jax import lax
from jax.sharding import PartitionSpec as P


def extended(shard, sides, width):
    for axis, dim in sides:
        devices, length = (lax.axis_size(axis), shard.shape[dim])
        up = [(i, (i + 1) % devices) for i in range(devices)]
        down = [(j, i) for i, j in up]
        last = lax.slice_in_dim(shard, length - width, length, axis=dim)
        leading = lax.slice_in_dim(shard, 0, width, axis=dim)
        before = lax.ppermute(last, axis, up)
        after = lax.ppermute(leading, axis, down)
        shard = jnp.concatenate([before, shard, after], axis=dim)
    return shard


def passed_along(shard, axis, by):
    devices = lax.axis_size(axis)
    return lax.ppermute(shard, axis, [(i, (i + by) % devices) for i in range(devices)])


def orient(block, mirrored):
    return jnp.where(mirrored == 1, block[..., ::-1], block)


def widen(active):
    gathered = lax.all_gather(active, "chan", axis=0, tiled=True)
    return extended(gathered, (("blk", 1),), 1)


def widen_by(active, before_rows, after_rows):
    gathered = lax.all_gather(active, "chan", axis=0, tiled=True)
    devices, length = lax.axis_size("blk"), gathered.shape[1]
    up = [(i, (i + 1) % devices) for i in range(devices)]
    down = [(j, i) for i, j in up]
    before = lax.ppermute(gathered[:, length - before_rows :], "blk", up)
    after = lax.ppermute(gathered[:, :after_rows], "blk", down)
    return jnp.concatenate([before, gathered, after], axis=1)


def conv_taps(padded, weight):
    row_count = padded.shape[1] - 2
    col_count = padded.shape[2]
    framed = jnp.pad(padded, ((0, 0), (0, 0), (1, 1)))
    running = jnp.zeros((weight.shape[2], row_count, col_count), jnp.float32)
    for row_tap in range(3):
        for col_tap in range(3):
            running = running + jnp.einsum(
                "oi,irw->orw",
                weight[row_tap, col_tap],
                framed[:, row_tap : row_tap + row_count, col_tap : col_tap + col_count],
                preferred_element_type=jnp.float32,
            )
    return running


def weight_taps(grad_out, padded):
    row_count = grad_out.shape[1]
    col_count = grad_out.shape[2]
    framed = jnp.pad(padded, ((0, 0), (0, 0), (1, 1)))
    stacked = []
    for row_tap in range(3):
        line = []
        for col_tap in range(3):
            line.append(
                jnp.einsum(
                    "orw,irw->oi",
                    grad_out,
                    framed[:, row_tap : row_tap + row_count, col_tap : col_tap + col_count],
                    preferred_element_type=jnp.float32,
                )
            )
        stacked.append(jnp.stack(line))
    return jnp.stack(stacked)


def spread_taps(grad_out, weight):
    row_count = grad_out.shape[1]
    col_count = grad_out.shape[2]
    framed = jnp.pad(grad_out, ((0, 0), (2, 2), (2, 2)))
    running = jnp.zeros((weight.shape[3], row_count + 2, col_count), jnp.float32)
    for row_tap in range(3):
        for col_tap in range(3):
            row_start = 2 - row_tap
            col_start = 3 - col_tap
            running = running + jnp.einsum(
                "oi,orw->irw",
                weight[row_tap, col_tap],
                framed[:, row_start : row_start + row_count + 2, col_start : col_start + col_count],
                preferred_element_type=jnp.float32,
            )
    return running


def spread_stride(grad_out, weight):
    out_rows = grad_out.shape[1]
    out_cols = grad_out.shape[2]
    channels = weight.shape[3]
    framed = jnp.pad(grad_out, ((0, 0), (1, 1), (1, 1)))
    parity_rows = []
    for row_par in range(2):
        parity_cols = []
        for col_par in range(2):
            running = jnp.zeros((channels, out_rows + 1, out_cols + 1), jnp.float32)
            for row_tap in range(row_par, 3, 2):
                for col_tap in range(col_par, 3, 2):
                    row_start = 1 - row_tap // 2
                    col_start = 1 - col_tap // 2
                    running = running + jnp.einsum(
                        "oi,orw->irw",
                        weight[row_tap, col_tap],
                        framed[
                            :,
                            row_start : row_start + out_rows + 1,
                            col_start : col_start + out_cols + 1,
                        ],
                        preferred_element_type=jnp.float32,
                    )
            parity_cols.append(running)
        parity_rows.append(jnp.stack(parity_cols, axis=3))
    woven = jnp.stack(parity_rows, axis=2)
    woven = woven.reshape(channels, 2 * out_rows + 2, 2 * out_cols + 2)
    return woven[:, : 2 * out_rows + 1, 1 : 2 * out_cols + 1]


def fold_rims(grad_rows, both_sides):
    interior = grad_rows[:, 1:-1] if both_sides else grad_rows[:, 1:]
    from_next = passed_along(grad_rows[:, :1].astype(jnp.bfloat16), "blk", -1).astype(jnp.float32)
    if both_sides:
        from_prev = passed_along(grad_rows[:, -1:].astype(jnp.bfloat16), "blk", 1).astype(
            jnp.float32
        )
        return jnp.concatenate(
            [interior[:, :1] + from_prev, interior[:, 1:-1], interior[:, -1:] + from_next], axis=1
        )
    return jnp.concatenate([interior[:, :-1], interior[:, -1:] + from_next], axis=1)


def own_inputs(weights):
    devices = lax.axis_size("chan")
    blocks = jnp.concatenate(weights, axis=2)
    blocks = blocks.reshape(blocks.shape[:3] + (devices, blocks.shape[3] // devices))
    swapped = lax.all_to_all(jnp.moveaxis(blocks, 3, 0), "chan", 0, 0, tiled=False)
    out, start = [], 0
    for w in weights:
        size = w.shape[2]
        out.append(jnp.concatenate([swapped[d, :, :, start : start + size] for d in range(devices)], axis=2))
        start += size
    return out


def input_grad(delta, weight):
    every = lax.all_gather(delta, "chan", axis=0, tiled=True)
    return fold_rims(spread_taps(every, weight), True)


def third_input_grad(upstream, weight):
    every = lax.all_gather(upstream, "chan", axis=0, tiled=True)
    return fold_rims(spread_stride(every, weight), False)


def parity_picker(cols, out_cols):
    source = lax.broadcasted_iota(jnp.int32, (cols, 3 * out_cols), 0)
    target = lax.broadcasted_iota(jnp.int32, (cols, 3 * out_cols), 1)
    wanted = 2 * (target % out_cols) + target // out_cols - 1
    return (source == wanted).astype(jnp.bfloat16)


def summed_over_cycle(parts, axis):
    devices = lax.axis_size(axis)
    flat = jnp.concatenate([p.reshape(-1) for p in parts])
    pieces = lax.all_to_all(flat.reshape(devices, -1), axis, 0, 0, tiled=True)
    total = jnp.sum(pieces, axis=0)
    spread = jnp.broadcast_to(total[None], (devices,) + total.shape)
    whole = lax.all_to_all(spread, axis, 0, 0, tiled=True).reshape(-1)
    out, start = [], 0
    for p in parts:
        out.append(whole[start : start + p.size].reshape(p.shape))
        start += p.size
    return out


def gelu_back(pre_act, grad_in):
    return jax.vjp(jax.nn.gelu, pre_act)[1](grad_in)[0]


def shards(inputs, w_first, w_second, w_third, cotangent, mirror):
    mirrored = mirror[0]
    oriented = orient(inputs, mirrored)
    upstream = orient(cotangent, mirrored)
    first_wide = widen_by(oriented, 3, 2)
    first_pre_wide = conv_taps(first_wide, w_first)
    first_act_wide = jax.nn.gelu(first_pre_wide).astype(jnp.bfloat16)
    first_pad = first_wide[:, 2:-1]
    first_pre = first_pre_wide[:, 2:-1]
    second_wide = lax.all_gather(first_act_wide, "chan", axis=0, tiled=True)
    second_pre_wide = conv_taps(second_wide, w_second)
    second_act_wide = jax.nn.gelu(second_pre_wide).astype(jnp.bfloat16)
    second_pad = second_wide[:, 1:]
    second_pre = second_pre_wide[:, 1:]
    stride_rows = lax.all_gather(second_act_wide, "chan", axis=0, tiled=True)
    out_rows = upstream.shape[1]
    out_cols = upstream.shape[2]
    by_parity = jnp.einsum(
        "irt,tk->irk",
        stride_rows,
        parity_picker(2 * out_cols, out_cols),
        preferred_element_type=jnp.float32,
    ).astype(jnp.bfloat16)
    spaced = jnp.stack([upstream, jnp.zeros_like(upstream)], axis=2).reshape(
        upstream.shape[0], 2 * out_rows, out_cols
    )
    row_placed = jnp.stack(
        [jnp.pad(spaced, ((0, 0), (row_tap, 1), (0, 0)))[:, : 2 * out_rows + 1] for row_tap in range(3)]
    )
    third_grad = jnp.stack(
        [
            jnp.einsum(
                "aosc,isc->aoi",
                row_placed,
                by_parity[:, :, col_tap * out_cols : (col_tap + 1) * out_cols],
                preferred_element_type=jnp.float32,
            )
            for col_tap in range(3)
        ],
        axis=1,
    )
    (third_mine,) = own_inputs((w_third,))
    first_mine, second_mine = own_inputs((w_first, w_second))
    second_back = third_input_grad(upstream, third_mine)
    second_delta = gelu_back(second_pre, second_back).astype(jnp.bfloat16)
    second_grad = weight_taps(second_delta, second_pad)
    first_back = input_grad(second_delta, second_mine)
    first_delta = gelu_back(first_pre, first_back).astype(jnp.bfloat16)
    first_grad = weight_taps(first_delta, first_pad)
    input_back = input_grad(first_delta, first_mine).astype(jnp.bfloat16)
    reduced = summed_over_cycle((first_grad, second_grad, third_grad), "blk")
    cell_count = inputs.shape[1] * inputs.shape[2] * lax.axis_size("blk")
    return (
        orient(input_back, mirrored),
        reduced[0] / math.sqrt(cell_count),
        reduced[1] / math.sqrt(cell_count),
        reduced[2] / math.sqrt(cell_count // 4),
    )


def solution(mesh):
    placed = (
        P("chan", "blk", None),
        P(None, None, "chan", None),
        P(None, None, "chan", None),
        P(None, None, "chan", None),
        P("chan", "blk", None),
        P("blk"),
    )
    return jax.shard_map(
        shards,
        mesh=mesh,
        in_specs=placed,
        out_specs=(
            P("chan", "blk", None),
            P(None, None, "chan", None),
            P(None, None, "chan", None),
            P(None, None, "chan", None),
        ),
        check_vma=False,
    )
```

```python
import math

import jax
import jax.numpy as jnp
from jax import lax
from jax.sharding import PartitionSpec as P


def extended(shard, sides, width):
    for axis, dim in sides:
        devices, length = (lax.axis_size(axis), shard.shape[dim])
        up = [(i, (i + 1) % devices) for i in range(devices)]
        down = [(j, i) for i, j in up]
        last = lax.slice_in_dim(shard, length - width, length, axis=dim)
        leading = lax.slice_in_dim(shard, 0, width, axis=dim)
        before = lax.ppermute(last, axis, up)
        after = lax.ppermute(leading, axis, down)
        shard = jnp.concatenate([before, shard, after], axis=dim)
    return shard


def passed_along(shard, axis, by):
    devices = lax.axis_size(axis)
    return lax.ppermute(shard, axis, [(i, (i + by) % devices) for i in range(devices)])


def orient(block, mirrored):
    return jnp.where(mirrored == 1, block[..., ::-1], block)


def widen(active):
    gathered = lax.all_gather(active, "chan", axis=0, tiled=True)
    return extended(gathered, (("blk", 1),), 1)


def widen_by(active, before_rows, after_rows):
    devices, length = lax.axis_size("blk"), active.shape[1]
    up = [(i, (i + 1) % devices) for i in range(devices)]
    down = [(j, i) for i, j in up]
    before = lax.ppermute(active[:, length - before_rows :], "blk", up)
    after = lax.ppermute(active[:, :after_rows], "blk", down)
    gathered = lax.all_gather(active, "chan", axis=0, tiled=True)
    rims = lax.all_gather(jnp.concatenate([before, after], axis=1), "chan", axis=0, tiled=True)
    return jnp.concatenate([rims[:, :before_rows], gathered, rims[:, before_rows:]], axis=1)


def conv_taps(padded, weight):
    row_count = padded.shape[1] - 2
    col_count = padded.shape[2]
    framed = jnp.pad(padded, ((0, 0), (0, 0), (1, 1)))
    running = jnp.zeros((weight.shape[2], row_count, col_count), jnp.float32)
    for row_tap in range(3):
        for col_tap in range(3):
            running = running + jnp.einsum(
                "oi,irw->orw",
                weight[row_tap, col_tap],
                framed[:, row_tap : row_tap + row_count, col_tap : col_tap + col_count],
                preferred_element_type=jnp.float32,
            )
    return running


def weight_taps(grad_out, padded):
    row_count = grad_out.shape[1]
    col_count = grad_out.shape[2]
    framed = jnp.pad(padded, ((0, 0), (0, 0), (1, 1)))
    stacked = []
    for row_tap in range(3):
        line = []
        for col_tap in range(3):
            line.append(
                jnp.einsum(
                    "orw,irw->oi",
                    grad_out,
                    framed[:, row_tap : row_tap + row_count, col_tap : col_tap + col_count],
                    preferred_element_type=jnp.float32,
                )
            )
        stacked.append(jnp.stack(line))
    return jnp.stack(stacked)


def spread_taps(grad_out, weight):
    row_count = grad_out.shape[1]
    col_count = grad_out.shape[2]
    framed = jnp.pad(grad_out, ((0, 0), (2, 2), (2, 2)))
    running = jnp.zeros((weight.shape[3], row_count + 2, col_count), jnp.float32)
    for row_tap in range(3):
        for col_tap in range(3):
            row_start = 2 - row_tap
            col_start = 3 - col_tap
            running = running + jnp.einsum(
                "oi,orw->irw",
                weight[row_tap, col_tap],
                framed[:, row_start : row_start + row_count + 2, col_start : col_start + col_count],
                preferred_element_type=jnp.float32,
            )
    return running


def spread_stride(grad_out, weight):
    out_rows = grad_out.shape[1]
    out_cols = grad_out.shape[2]
    channels = weight.shape[3]
    framed = jnp.pad(grad_out, ((0, 0), (1, 1), (1, 1)))
    parity_rows = []
    for row_par in range(2):
        parity_cols = []
        for col_par in range(2):
            running = jnp.zeros((channels, out_rows + 1, out_cols + 1), jnp.float32)
            for row_tap in range(row_par, 3, 2):
                for col_tap in range(col_par, 3, 2):
                    row_start = 1 - row_tap // 2
                    col_start = 1 - col_tap // 2
                    running = running + jnp.einsum(
                        "oi,orw->irw",
                        weight[row_tap, col_tap],
                        framed[
                            :,
                            row_start : row_start + out_rows + 1,
                            col_start : col_start + out_cols + 1,
                        ],
                        preferred_element_type=jnp.float32,
                    )
            parity_cols.append(running)
        parity_rows.append(jnp.stack(parity_cols, axis=3))
    woven = jnp.stack(parity_rows, axis=2)
    woven = woven.reshape(channels, 2 * out_rows + 2, 2 * out_cols + 2)
    return woven[:, : 2 * out_rows + 1, 1 : 2 * out_cols + 1]


def fold_rims(grad_rows, both_sides):
    interior = grad_rows[:, 1:-1] if both_sides else grad_rows[:, 1:]
    from_next = passed_along(grad_rows[:, :1].astype(jnp.bfloat16), "blk", -1).astype(jnp.float32)
    if both_sides:
        from_prev = passed_along(grad_rows[:, -1:].astype(jnp.bfloat16), "blk", 1).astype(
            jnp.float32
        )
        return jnp.concatenate(
            [interior[:, :1] + from_prev, interior[:, 1:-1], interior[:, -1:] + from_next], axis=1
        )
    return jnp.concatenate([interior[:, :-1], interior[:, -1:] + from_next], axis=1)


def own_inputs(weight):
    whole = lax.all_gather(weight, "chan", axis=2, tiled=True)
    width = whole.shape[3] // lax.axis_size("chan")
    return lax.dynamic_slice_in_dim(whole, lax.axis_index("chan") * width, width, axis=3)


def input_grad(delta, weight):
    every = lax.all_gather(delta, "chan", axis=0, tiled=True)
    return fold_rims(spread_taps(every, weight), True)


def third_input_grad(upstream, weight):
    every = lax.all_gather(upstream, "chan", axis=0, tiled=True)
    return fold_rims(spread_stride(every, weight), False)


def parity_picker(cols, out_cols):
    source = lax.broadcasted_iota(jnp.int32, (cols, 3 * out_cols), 0)
    target = lax.broadcasted_iota(jnp.int32, (cols, 3 * out_cols), 1)
    wanted = 2 * (target % out_cols) + target // out_cols - 1
    return (source == wanted).astype(jnp.bfloat16)


def summed_over_cycle(parts, axis):
    devices = lax.axis_size(axis)
    flat = jnp.concatenate([p.reshape(-1) for p in parts])
    pieces = lax.all_to_all(flat.reshape(devices, -1), axis, 0, 0, tiled=True)
    total = jnp.sum(pieces, axis=0)
    spread = jnp.broadcast_to(total[None], (devices,) + total.shape)
    whole = lax.all_to_all(spread, axis, 0, 0, tiled=True).reshape(-1)
    out, start = [], 0
    for p in parts:
        out.append(whole[start : start + p.size].reshape(p.shape))
        start += p.size
    return out


def gelu_back(pre_act, grad_in):
    return jax.vjp(jax.nn.gelu, pre_act)[1](grad_in)[0]


def shards(inputs, w_first, w_second, w_third, cotangent, mirror):
    mirrored = mirror[0]
    oriented = orient(inputs, mirrored)
    upstream = orient(cotangent, mirrored)
    first_wide = widen_by(oriented, 3, 2)
    first_pre_wide = conv_taps(first_wide, w_first)
    first_act_wide = jax.nn.gelu(first_pre_wide).astype(jnp.bfloat16)
    first_pad = first_wide[:, 2:-1]
    first_pre = first_pre_wide[:, 2:-1]
    second_wide = lax.all_gather(first_act_wide, "chan", axis=0, tiled=True)
    second_pre_wide = conv_taps(second_wide, w_second)
    second_act_wide = jax.nn.gelu(second_pre_wide).astype(jnp.bfloat16)
    second_pad = second_wide[:, 1:]
    second_pre = second_pre_wide[:, 1:]
    stride_rows = lax.all_gather(second_act_wide, "chan", axis=0, tiled=True)
    out_rows = upstream.shape[1]
    out_cols = upstream.shape[2]
    by_parity = jnp.einsum(
        "irt,tk->irk",
        stride_rows,
        parity_picker(2 * out_cols, out_cols),
        preferred_element_type=jnp.float32,
    ).astype(jnp.bfloat16)
    spaced = jnp.stack([upstream, jnp.zeros_like(upstream)], axis=2).reshape(
        upstream.shape[0], 2 * out_rows, out_cols
    )
    row_placed = jnp.stack(
        [jnp.pad(spaced, ((0, 0), (row_tap, 1), (0, 0)))[:, : 2 * out_rows + 1] for row_tap in range(3)]
    )
    third_grad = jnp.stack(
        [
            jnp.einsum(
                "aosc,isc->aoi",
                row_placed,
                by_parity[:, :, col_tap * out_cols : (col_tap + 1) * out_cols],
                preferred_element_type=jnp.float32,
            )
            for col_tap in range(3)
        ],
        axis=1,
    )
    second_back = third_input_grad(upstream, own_inputs(w_third))
    second_delta = gelu_back(second_pre, second_back).astype(jnp.bfloat16)
    second_grad = weight_taps(second_delta, second_pad)
    first_back = input_grad(second_delta, own_inputs(w_second))
    first_delta = gelu_back(first_pre, first_back).astype(jnp.bfloat16)
    first_grad = weight_taps(first_delta, first_pad)
    input_back = input_grad(first_delta, own_inputs(w_first)).astype(jnp.bfloat16)
    reduced = summed_over_cycle((first_grad, second_grad, third_grad), "blk")
    cell_count = inputs.shape[1] * inputs.shape[2] * lax.axis_size("blk")
    return (
        orient(input_back, mirrored),
        reduced[0] / math.sqrt(cell_count),
        reduced[1] / math.sqrt(cell_count),
        reduced[2] / math.sqrt(cell_count // 4),
    )


def solution(mesh):
    placed = (
        P("chan", "blk", None),
        P(None, None, "chan", None),
        P(None, None, "chan", None),
        P(None, None, "chan", None),
        P("chan", "blk", None),
        P("blk"),
    )
    return jax.shard_map(
        shards,
        mesh=mesh,
        in_specs=placed,
        out_specs=(
            P("chan", "blk", None),
            P(None, None, "chan", None),
            P(None, None, "chan", None),
            P(None, None, "chan", None),
        ),
        check_vma=False,
    )
```

```python
import math

import jax
import jax.numpy as jnp
from jax import lax
from jax.sharding import PartitionSpec as P


def extended(shard, sides, width):
    for axis, dim in sides:
        devices, length = (lax.axis_size(axis), shard.shape[dim])
        up = [(i, (i + 1) % devices) for i in range(devices)]
        down = [(j, i) for i, j in up]
        last = lax.slice_in_dim(shard, length - width, length, axis=dim)
        leading = lax.slice_in_dim(shard, 0, width, axis=dim)
        before = lax.ppermute(last, axis, up)
        after = lax.ppermute(leading, axis, down)
        shard = jnp.concatenate([before, shard, after], axis=dim)
    return shard


def passed_along(shard, axis, by):
    devices = lax.axis_size(axis)
    return lax.ppermute(shard, axis, [(i, (i + by) % devices) for i in range(devices)])


def orient(block, mirrored):
    return jnp.where(mirrored == 1, block[..., ::-1], block)


def widen(active):
    gathered = lax.all_gather(active, "chan", axis=0, tiled=True)
    return extended(gathered, (("blk", 1),), 1)


def widen_by(active, before_rows, after_rows):
    gathered = lax.all_gather(active, "chan", axis=0, tiled=True)
    devices, length = lax.axis_size("blk"), gathered.shape[1]
    up = [(i, (i + 1) % devices) for i in range(devices)]
    down = [(j, i) for i, j in up]
    before = lax.ppermute(gathered[:, length - before_rows :], "blk", up)
    after = lax.ppermute(gathered[:, :after_rows], "blk", down)
    return jnp.concatenate([before, gathered, after], axis=1)


def conv_taps(padded, weight):
    row_count = padded.shape[1] - 2
    col_count = padded.shape[2]
    framed = jnp.pad(padded, ((0, 0), (0, 0), (1, 1)))
    running = jnp.zeros((weight.shape[2], row_count, col_count), jnp.float32)
    for row_tap in range(3):
        for col_tap in range(3):
            running = running + jnp.einsum(
                "oi,irw->orw",
                weight[row_tap, col_tap],
                framed[:, row_tap : row_tap + row_count, col_tap : col_tap + col_count],
                preferred_element_type=jnp.float32,
            )
    return running


def weight_taps(grad_out, padded):
    row_count = grad_out.shape[1]
    col_count = grad_out.shape[2]
    framed = jnp.pad(padded, ((0, 0), (0, 0), (1, 1)))
    views = jnp.stack(
        [
            framed[:, row_tap : row_tap + row_count, col_tap : col_tap + col_count]
            for row_tap in range(3)
            for col_tap in range(3)
        ]
    )
    taps = jnp.einsum("orw,kirw->koi", grad_out, views, preferred_element_type=jnp.float32)
    return taps.reshape((3, 3) + taps.shape[1:])


def spread_taps(grad_out, weight):
    row_count = grad_out.shape[1]
    col_count = grad_out.shape[2]
    framed = jnp.pad(grad_out, ((0, 0), (2, 2), (2, 2)))
    running = jnp.zeros((weight.shape[3], row_count + 2, col_count), jnp.float32)
    for row_tap in range(3):
        for col_tap in range(3):
            row_start = 2 - row_tap
            col_start = 3 - col_tap
            running = running + jnp.einsum(
                "oi,orw->irw",
                weight[row_tap, col_tap],
                framed[:, row_start : row_start + row_count + 2, col_start : col_start + col_count],
                preferred_element_type=jnp.float32,
            )
    return running


def spread_stride(grad_out, weight):
    out_rows = grad_out.shape[1]
    out_cols = grad_out.shape[2]
    channels = weight.shape[3]
    framed = jnp.pad(grad_out, ((0, 0), (1, 1), (1, 1)))
    parity_rows = []
    for row_par in range(2):
        parity_cols = []
        for col_par in range(2):
            running = jnp.zeros((channels, out_rows + 1, out_cols + 1), jnp.float32)
            for row_tap in range(row_par, 3, 2):
                for col_tap in range(col_par, 3, 2):
                    row_start = 1 - row_tap // 2
                    col_start = 1 - col_tap // 2
                    running = running + jnp.einsum(
                        "oi,orw->irw",
                        weight[row_tap, col_tap],
                        framed[
                            :,
                            row_start : row_start + out_rows + 1,
                            col_start : col_start + out_cols + 1,
                        ],
                        preferred_element_type=jnp.float32,
                    )
            parity_cols.append(running)
        parity_rows.append(jnp.stack(parity_cols, axis=3))
    woven = jnp.stack(parity_rows, axis=2)
    woven = woven.reshape(channels, 2 * out_rows + 2, 2 * out_cols + 2)
    return woven[:, : 2 * out_rows + 1, 1 : 2 * out_cols + 1]


def fold_rims(grad_rows, both_sides):
    interior = grad_rows[:, 1:-1] if both_sides else grad_rows[:, 1:]
    from_next = passed_along(grad_rows[:, :1].astype(jnp.bfloat16), "blk", -1).astype(jnp.float32)
    if both_sides:
        from_prev = passed_along(grad_rows[:, -1:].astype(jnp.bfloat16), "blk", 1).astype(
            jnp.float32
        )
        return jnp.concatenate(
            [interior[:, :1] + from_prev, interior[:, 1:-1], interior[:, -1:] + from_next], axis=1
        )
    return jnp.concatenate([interior[:, :-1], interior[:, -1:] + from_next], axis=1)


def own_inputs(weight):
    whole = lax.all_gather(weight, "chan", axis=2, tiled=True)
    width = whole.shape[3] // lax.axis_size("chan")
    return lax.dynamic_slice_in_dim(whole, lax.axis_index("chan") * width, width, axis=3)


def input_grad(delta, weight):
    every = lax.all_gather(delta, "chan", axis=0, tiled=True)
    return fold_rims(spread_taps(every, weight), True)


def third_input_grad(upstream, weight):
    every = lax.all_gather(upstream, "chan", axis=0, tiled=True)
    return fold_rims(spread_stride(every, weight), False)


def parity_picker(cols, out_cols):
    source = lax.broadcasted_iota(jnp.int32, (cols, 3 * out_cols), 0)
    target = lax.broadcasted_iota(jnp.int32, (cols, 3 * out_cols), 1)
    wanted = 2 * (target % out_cols) + target // out_cols - 1
    return (source == wanted).astype(jnp.bfloat16)


def summed_over_cycle(parts, axis):
    devices = lax.axis_size(axis)
    flat = jnp.concatenate([p.reshape(-1) for p in parts])
    pieces = lax.all_to_all(flat.reshape(devices, -1), axis, 0, 0, tiled=True)
    total = jnp.sum(pieces, axis=0)
    spread = jnp.broadcast_to(total[None], (devices,) + total.shape)
    whole = lax.all_to_all(spread, axis, 0, 0, tiled=True).reshape(-1)
    out, start = [], 0
    for p in parts:
        out.append(whole[start : start + p.size].reshape(p.shape))
        start += p.size
    return out


def gelu_back(pre_act, grad_in):
    return jax.vjp(jax.nn.gelu, pre_act)[1](grad_in)[0]


def shards(inputs, w_first, w_second, w_third, cotangent, mirror):
    mirrored = mirror[0]
    oriented = orient(inputs, mirrored)
    upstream = orient(cotangent, mirrored)
    first_wide = widen_by(oriented, 3, 2)
    first_pre_wide = conv_taps(first_wide, w_first)
    first_act_wide = jax.nn.gelu(first_pre_wide).astype(jnp.bfloat16)
    first_pad = first_wide[:, 2:-1]
    first_pre = first_pre_wide[:, 2:-1]
    second_wide = lax.all_gather(first_act_wide, "chan", axis=0, tiled=True)
    second_pre_wide = conv_taps(second_wide, w_second)
    second_act_wide = jax.nn.gelu(second_pre_wide).astype(jnp.bfloat16)
    second_pad = second_wide[:, 1:]
    second_pre = second_pre_wide[:, 1:]
    stride_rows = lax.all_gather(second_act_wide, "chan", axis=0, tiled=True)
    out_rows = upstream.shape[1]
    out_cols = upstream.shape[2]
    by_parity = jnp.einsum(
        "irt,tk->irk",
        stride_rows,
        parity_picker(2 * out_cols, out_cols),
        preferred_element_type=jnp.float32,
    ).astype(jnp.bfloat16)
    spaced = jnp.stack([upstream, jnp.zeros_like(upstream)], axis=2).reshape(
        upstream.shape[0], 2 * out_rows, out_cols
    )
    row_placed = jnp.stack(
        [jnp.pad(spaced, ((0, 0), (row_tap, 1), (0, 0)))[:, : 2 * out_rows + 1] for row_tap in range(3)]
    )
    third_grad = jnp.stack(
        [
            jnp.einsum(
                "aosc,isc->aoi",
                row_placed,
                by_parity[:, :, col_tap * out_cols : (col_tap + 1) * out_cols],
                preferred_element_type=jnp.float32,
            )
            for col_tap in range(3)
        ],
        axis=1,
    )
    second_back = third_input_grad(upstream, own_inputs(w_third))
    second_delta = gelu_back(second_pre, second_back).astype(jnp.bfloat16)
    second_grad = weight_taps(second_delta, second_pad)
    first_back = input_grad(second_delta, own_inputs(w_second))
    first_delta = gelu_back(first_pre, first_back).astype(jnp.bfloat16)
    first_grad = weight_taps(first_delta, first_pad)
    input_back = input_grad(first_delta, own_inputs(w_first)).astype(jnp.bfloat16)
    reduced = summed_over_cycle((first_grad, second_grad, third_grad), "blk")
    cell_count = inputs.shape[1] * inputs.shape[2] * lax.axis_size("blk")
    return (
        orient(input_back, mirrored),
        reduced[0] / math.sqrt(cell_count),
        reduced[1] / math.sqrt(cell_count),
        reduced[2] / math.sqrt(cell_count // 4),
    )


def solution(mesh):
    placed = (
        P("chan", "blk", None),
        P(None, None, "chan", None),
        P(None, None, "chan", None),
        P(None, None, "chan", None),
        P("chan", "blk", None),
        P("blk"),
    )
    return jax.shard_map(
        shards,
        mesh=mesh,
        in_specs=placed,
        out_specs=(
            P("chan", "blk", None),
            P(None, None, "chan", None),
            P(None, None, "chan", None),
            P(None, None, "chan", None),
        ),
        check_vma=False,
    )
```

```python
import math

import jax
import jax.numpy as jnp
from jax import lax
from jax.sharding import PartitionSpec as P


def extended(shard, sides, width):
    for axis, dim in sides:
        devices, length = (lax.axis_size(axis), shard.shape[dim])
        up = [(i, (i + 1) % devices) for i in range(devices)]
        down = [(j, i) for i, j in up]
        last = lax.slice_in_dim(shard, length - width, length, axis=dim)
        leading = lax.slice_in_dim(shard, 0, width, axis=dim)
        before = lax.ppermute(last, axis, up)
        after = lax.ppermute(leading, axis, down)
        shard = jnp.concatenate([before, shard, after], axis=dim)
    return shard


def passed_along(shard, axis, by):
    devices = lax.axis_size(axis)
    return lax.ppermute(shard, axis, [(i, (i + by) % devices) for i in range(devices)])


def orient(block, mirrored):
    return jnp.where(mirrored == 1, block[..., ::-1], block)


def widen(active):
    gathered = lax.all_gather(active, "chan", axis=0, tiled=True)
    return extended(gathered, (("blk", 1),), 1)


def widen_by(active, before_rows, after_rows):
    gathered = lax.all_gather(active, "chan", axis=0, tiled=True)
    devices, length = lax.axis_size("blk"), gathered.shape[1]
    up = [(i, (i + 1) % devices) for i in range(devices)]
    down = [(j, i) for i, j in up]
    before = lax.ppermute(gathered[:, length - before_rows :], "blk", up)
    after = lax.ppermute(gathered[:, :after_rows], "blk", down)
    return jnp.concatenate([before, gathered, after], axis=1)


def conv_taps(padded, weight):
    row_count = padded.shape[1] - 2
    col_count = padded.shape[2]
    framed = jnp.pad(padded, ((0, 0), (0, 0), (1, 1)))
    running = jnp.zeros((weight.shape[2], row_count, col_count), jnp.float32)
    for row_tap in range(3):
        for col_tap in range(3):
            running = running + jnp.einsum(
                "oi,irw->orw",
                weight[row_tap, col_tap],
                framed[:, row_tap : row_tap + row_count, col_tap : col_tap + col_count],
                preferred_element_type=jnp.float32,
            )
    return running


def weight_taps(grad_out, padded):
    row_count = grad_out.shape[1]
    col_count = grad_out.shape[2]
    framed = jnp.pad(padded, ((0, 0), (0, 0), (1, 1)))
    views = jnp.stack(
        [
            framed[:, row_tap : row_tap + row_count, col_tap : col_tap + col_count]
            for row_tap in range(3)
            for col_tap in range(3)
        ]
    )
    taps = jnp.einsum("orw,kirw->koi", grad_out, views, preferred_element_type=jnp.float32)
    return taps.reshape((3, 3) + taps.shape[1:])


def spread_taps(grad_out, weight):
    row_count = grad_out.shape[1]
    col_count = grad_out.shape[2]
    framed = jnp.pad(grad_out, ((0, 0), (2, 2), (2, 2)))
    views = jnp.stack(
        [
            framed[:, 2 - row_tap : 4 - row_tap + row_count, 3 - col_tap : 3 - col_tap + col_count]
            for row_tap in range(3)
            for col_tap in range(3)
        ]
    )
    taps = weight.reshape((9,) + weight.shape[2:])
    return jnp.einsum("koi,korw->irw", taps, views, preferred_element_type=jnp.float32)


def spread_stride(grad_out, weight):
    out_rows = grad_out.shape[1]
    out_cols = grad_out.shape[2]
    channels = weight.shape[3]
    framed = jnp.pad(grad_out, ((0, 0), (1, 1), (1, 1)))
    parity_rows = []
    for row_par in range(2):
        parity_cols = []
        for col_par in range(2):
            running = jnp.zeros((channels, out_rows + 1, out_cols + 1), jnp.float32)
            for row_tap in range(row_par, 3, 2):
                for col_tap in range(col_par, 3, 2):
                    row_start = 1 - row_tap // 2
                    col_start = 1 - col_tap // 2
                    running = running + jnp.einsum(
                        "oi,orw->irw",
                        weight[row_tap, col_tap],
                        framed[
                            :,
                            row_start : row_start + out_rows + 1,
                            col_start : col_start + out_cols + 1,
                        ],
                        preferred_element_type=jnp.float32,
                    )
            parity_cols.append(running)
        parity_rows.append(jnp.stack(parity_cols, axis=3))
    woven = jnp.stack(parity_rows, axis=2)
    woven = woven.reshape(channels, 2 * out_rows + 2, 2 * out_cols + 2)
    return woven[:, : 2 * out_rows + 1, 1 : 2 * out_cols + 1]


def fold_rims(grad_rows, both_sides):
    interior = grad_rows[:, 1:-1] if both_sides else grad_rows[:, 1:]
    from_next = passed_along(grad_rows[:, :1].astype(jnp.bfloat16), "blk", -1).astype(jnp.float32)
    if both_sides:
        from_prev = passed_along(grad_rows[:, -1:].astype(jnp.bfloat16), "blk", 1).astype(
            jnp.float32
        )
        return jnp.concatenate(
            [interior[:, :1] + from_prev, interior[:, 1:-1], interior[:, -1:] + from_next], axis=1
        )
    return jnp.concatenate([interior[:, :-1], interior[:, -1:] + from_next], axis=1)


def own_inputs(weight):
    whole = lax.all_gather(weight, "chan", axis=2, tiled=True)
    width = whole.shape[3] // lax.axis_size("chan")
    return lax.dynamic_slice_in_dim(whole, lax.axis_index("chan") * width, width, axis=3)


def input_grad(delta, weight):
    every = lax.all_gather(delta, "chan", axis=0, tiled=True)
    return fold_rims(spread_taps(every, weight), True)


def third_input_grad(upstream, weight):
    every = lax.all_gather(upstream, "chan", axis=0, tiled=True)
    return fold_rims(spread_stride(every, weight), False)


def parity_picker(cols, out_cols):
    source = lax.broadcasted_iota(jnp.int32, (cols, 3 * out_cols), 0)
    target = lax.broadcasted_iota(jnp.int32, (cols, 3 * out_cols), 1)
    wanted = 2 * (target % out_cols) + target // out_cols - 1
    return (source == wanted).astype(jnp.bfloat16)


def summed_over_cycle(parts, axis):
    devices = lax.axis_size(axis)
    flat = jnp.concatenate([p.reshape(-1) for p in parts])
    pieces = lax.all_to_all(flat.reshape(devices, -1), axis, 0, 0, tiled=True)
    total = jnp.sum(pieces, axis=0)
    spread = jnp.broadcast_to(total[None], (devices,) + total.shape)
    whole = lax.all_to_all(spread, axis, 0, 0, tiled=True).reshape(-1)
    out, start = [], 0
    for p in parts:
        out.append(whole[start : start + p.size].reshape(p.shape))
        start += p.size
    return out


def gelu_back(pre_act, grad_in):
    return jax.vjp(jax.nn.gelu, pre_act)[1](grad_in)[0]


def shards(inputs, w_first, w_second, w_third, cotangent, mirror):
    mirrored = mirror[0]
    oriented = orient(inputs, mirrored)
    upstream = orient(cotangent, mirrored)
    first_wide = widen_by(oriented, 3, 2)
    first_pre_wide = conv_taps(first_wide, w_first)
    first_act_wide = jax.nn.gelu(first_pre_wide).astype(jnp.bfloat16)
    first_pad = first_wide[:, 2:-1]
    first_pre = first_pre_wide[:, 2:-1]
    second_wide = lax.all_gather(first_act_wide, "chan", axis=0, tiled=True)
    second_pre_wide = conv_taps(second_wide, w_second)
    second_act_wide = jax.nn.gelu(second_pre_wide).astype(jnp.bfloat16)
    second_pad = second_wide[:, 1:]
    second_pre = second_pre_wide[:, 1:]
    stride_rows = lax.all_gather(second_act_wide, "chan", axis=0, tiled=True)
    out_rows = upstream.shape[1]
    out_cols = upstream.shape[2]
    by_parity = jnp.einsum(
        "irt,tk->irk",
        stride_rows,
        parity_picker(2 * out_cols, out_cols),
        preferred_element_type=jnp.float32,
    ).astype(jnp.bfloat16)
    spaced = jnp.stack([upstream, jnp.zeros_like(upstream)], axis=2).reshape(
        upstream.shape[0], 2 * out_rows, out_cols
    )
    row_placed = jnp.stack(
        [jnp.pad(spaced, ((0, 0), (row_tap, 1), (0, 0)))[:, : 2 * out_rows + 1] for row_tap in range(3)]
    )
    third_grad = jnp.stack(
        [
            jnp.einsum(
                "aosc,isc->aoi",
                row_placed,
                by_parity[:, :, col_tap * out_cols : (col_tap + 1) * out_cols],
                preferred_element_type=jnp.float32,
            )
            for col_tap in range(3)
        ],
        axis=1,
    )
    second_back = third_input_grad(upstream, own_inputs(w_third))
    second_delta = gelu_back(second_pre, second_back).astype(jnp.bfloat16)
    second_grad = weight_taps(second_delta, second_pad)
    first_back = input_grad(second_delta, own_inputs(w_second))
    first_delta = gelu_back(first_pre, first_back).astype(jnp.bfloat16)
    first_grad = weight_taps(first_delta, first_pad)
    input_back = input_grad(first_delta, own_inputs(w_first)).astype(jnp.bfloat16)
    reduced = summed_over_cycle((first_grad, second_grad, third_grad), "blk")
    cell_count = inputs.shape[1] * inputs.shape[2] * lax.axis_size("blk")
    return (
        orient(input_back, mirrored),
        reduced[0] / math.sqrt(cell_count),
        reduced[1] / math.sqrt(cell_count),
        reduced[2] / math.sqrt(cell_count // 4),
    )


def solution(mesh):
    placed = (
        P("chan", "blk", None),
        P(None, None, "chan", None),
        P(None, None, "chan", None),
        P(None, None, "chan", None),
        P("chan", "blk", None),
        P("blk"),
    )
    return jax.shard_map(
        shards,
        mesh=mesh,
        in_specs=placed,
        out_specs=(
            P("chan", "blk", None),
            P(None, None, "chan", None),
            P(None, None, "chan", None),
            P(None, None, "chan", None),
        ),
        check_vma=False,
    )
```
